32 devices in a mesh: groups: 2 (over y), seq: 4 (over z), head: 2 (over x), sub: 2 (over core).
Axes of the slice: x: 2, y: 2, z: 4, core: 2. Of those that a mesh axis runs over, the one named last changes fastest.
Arguments:
- tokens: bfloat16 [4096, 3072], P(('groups', 'seq')), parts along dimension 0, may hold values from -6 to 6
- modulation: float32 [3, 3072], replicated, may hold values from -4 to 4
- w_qkv: bfloat16 [3072, 8, 768], P('seq', ('head', 'sub')), may hold values from -0.15625 to 0.15625
- w_out: bfloat16 [2048, 3072], P('seq', ('head', 'sub')), may hold values from -0.125 to 0.125
- pattern: int32 [32, 4], P(('groups', 'seq')), parts along dimension 0, may hold values from 0 to 15, as said below
- counts: int32 [32], P(('groups', 'seq')), parts along dimension 0, may hold values from 1 to 4, as said below
- spatial_mask: int32 [8, 4, 4], P(('groups', 'seq')), parts along dimension 0, may hold values from 0 to 1, as said below
Outputs:
- update: bfloat16 [4096, 3072], P(('groups', 'seq'), ('head', 'sub')), parts along dimension 0
The draws below stay inside these ranges and needn't reach their ends.
There are 2 independent parts, one for each index of `groups`. The reference program is written for one: setup_inputs(seed, part) draws one part's arguments, and reference() takes and returns one part's arrays. A program takes and returns all parts, laid end to end along the dimension named above; an argument that names none is the same for every part. Nothing has to cross between parts.
Inputs may be any that keep to these rules, and one draw needn't show every extreme that they name: pattern[b, 0] = b; each further entry of row b is b plus a nonzero offset of size at most 2, the offsets of one row different, clipped to the blocks of the video. `counts`: blocks with a count above one all lie in one cyclic run of half of the 16 blocks. `spatial_mask`: every diagonal entry is 1.
All inputs are finite; a program needn't handle non-finite values.
Results may differ from the reference program's by a relative error of at most 0.012.
The reference program's roundings to bfloat16 on the way count: a program that leaves them out, or rounds other values in their place, can miss the bound.
Values may be sent and summed in bfloat16 or wider, within the bound.
A program may use at most 128 MiB of HBM per device.

```python
import math
import jax
import jax.numpy as jnp
from jax import lax

D = 3072
HD = 128
PAIRS = 8
BLOCK = 128
WIN = 2
SLOTS = 4
POS = 512
FRAMES = 4
ROWS = 2048
TB = 16
SB = 4


def draw_pattern(key, part):
    blocks = jnp.arange(TB, dtype=jnp.int32)
    scores = jax.random.randint(jax.random.fold_in(key, 11), (TB, 2 * WIN), 0, 4096, dtype=jnp.int32)
    scores = scores * (2 * WIN) + jnp.arange(2 * WIN, dtype=jnp.int32)[None, :]
    order = jnp.argsort(scores, axis=1)
    offset_table = jnp.concatenate([jnp.arange(-WIN, 0, dtype=jnp.int32), jnp.arange(1, WIN + 1, dtype=jnp.int32)])
    chosen = offset_table[order[:, :SLOTS - 1]]
    others = jnp.clip(blocks[:, None] + chosen, 0, TB - 1)
    return jnp.concatenate([blocks[:, None], others], axis=1).astype(jnp.int32)


def draw_counts(key, part):
    blocks = jnp.arange(TB, dtype=jnp.int32)
    first_hot = jax.random.randint(jax.random.fold_in(key, 21), (), 0, TB, dtype=jnp.int32)
    inside = (blocks - first_hot) % TB < TB // 2
    level = jax.random.randint(jax.random.fold_in(key, 22), (TB,), 1, SLOTS + 1, dtype=jnp.int32)
    values = jnp.where(inside, level, 1)
    return jnp.where(blocks == first_hot, SLOTS, values).astype(jnp.int32)


def draw_spatial_mask(key, part):
    random_bits = jax.random.randint(jax.random.fold_in(key, 31), (FRAMES, SB, SB), 0, 2, dtype=jnp.int32)
    diagonal = (jnp.arange(SB, dtype=jnp.int32)[:, None] == jnp.arange(SB, dtype=jnp.int32)[None, :]).astype(jnp.int32)
    return jnp.maximum(random_bits, diagonal[None, :, :]).astype(jnp.int32)


def levels(stream_key, extent, pieces, least, top_value):
    gain = 1.0
    for dim, shards_of in pieces:
        heights = jax.random.uniform(jax.random.fold_in(jax.random.fold_in(stream_key, 6), dim), (shards_of,), jnp.float32, least / len(pieces), top_value / len(pieces))
        gain = gain * jnp.repeat(jnp.exp(heights), extent[dim] // shards_of).reshape((-1,) + (1,) * (len(extent) - 1 - dim))
    return gain


def bell_draw(rng, dims, width, bound, split=(), kind=jnp.bfloat16):
    drawn = width * jax.random.normal(rng, dims, jnp.float32)
    if split:
        drawn = drawn * levels(rng, dims, split, -0.22, 0.18)
    return jnp.clip(drawn, -bound, bound).astype(kind)


def setup_inputs(seed: int = 0, part: int = 0) -> dict:
    splits = jax.random.split(jax.random.key(seed), 8)
    own_keys = jax.random.split(jax.random.fold_in(splits[7], part), 8)
    return {
        "tokens": bell_draw(own_keys[0], (ROWS, D), 1.0, 6.0, ((0, 4),)),
        "modulation": bell_draw(splits[1], (3, D), 1.0, 4.0, (), jnp.float32),
        "w_qkv": bell_draw(splits[2], (D, PAIRS, 6 * HD), (D // 2) ** -0.5, 0.15625, ((0, 4), (1, 4))),
        "w_out": bell_draw(splits[3], (2 * PAIRS * HD, D), (2 * PAIRS * HD) ** -0.5, 0.125, ((0, 4), (1, 4))),
        "pattern": draw_pattern(jax.random.fold_in(jax.random.fold_in(splits[7], part), 71), part),
        "counts": draw_counts(jax.random.fold_in(jax.random.fold_in(splits[7], part), 71), part),
        "spatial_mask": draw_spatial_mask(jax.random.fold_in(jax.random.fold_in(splits[7], part), 71), part),
    }


EPSILON = 1e-06

def modulate(tokens, modulation):
    values = tokens.astype(jnp.float32)
    center = lax.optimization_barrier(jnp.mean(values, axis=-1, keepdims=True))
    spread = lax.optimization_barrier(jnp.mean(jnp.square(values - center), axis=-1, keepdims=True))
    normed = (values - center) * lax.rsqrt(spread + EPSILON)
    return (normed * (1.0 + modulation[1]) + modulation[0]).astype(jnp.bfloat16)

def pair_attention(hidden, weight, pattern, counts, spatial_mask):
    scale_factor = 1.0 / math.sqrt(HD)
    qkv = jnp.dot(hidden, weight, preferred_element_type=jnp.float32).astype(jnp.bfloat16)
    temporal = qkv[:, :3 * HD].reshape(FRAMES, POS, 3 * HD).transpose(1, 0, 2).reshape(TB, BLOCK, 3 * HD)
    queries = temporal[:, :, :HD].astype(jnp.float32)
    key_blocks = temporal[:, :, HD:2 * HD][pattern].astype(jnp.float32)
    value_blocks = temporal[:, :, 2 * HD:][pattern].astype(jnp.float32)
    scores = jnp.einsum('bqc,bjkc->bjqk', queries, key_blocks) * scale_factor
    alive = (jnp.arange(SLOTS, dtype=jnp.int32)[None, :] < counts[:, None]).astype(jnp.float32)
    weights = jnp.exp(scores) * alive[:, :, None, None]
    denominator = lax.optimization_barrier(jnp.sum(weights, axis=(1, 3)))
    rounded = lax.optimization_barrier(weights.astype(jnp.bfloat16)).astype(jnp.float32)
    numerator = jnp.einsum('bjqk,bjkc->bqc', rounded, value_blocks)
    temporal_out = (numerator / denominator[:, :, None]).astype(jnp.bfloat16)
    temporal_out = temporal_out.reshape(POS, FRAMES, HD).transpose(1, 0, 2).reshape(ROWS, HD)
    spatial = qkv[:, 3 * HD:].reshape(FRAMES, POS, 3 * HD).astype(jnp.float32)
    scores = jnp.einsum('fpc,fqc->fpq', spatial[..., :HD], spatial[..., HD:2 * HD]) * scale_factor
    keep = spatial_mask.astype(jnp.float32)[:, :, None, :, None]
    weights = (jnp.exp(scores).reshape(FRAMES, SB, BLOCK, SB, BLOCK) * keep).reshape(FRAMES, POS, POS)
    denominator = lax.optimization_barrier(jnp.sum(weights, axis=-1))
    rounded = lax.optimization_barrier(weights.astype(jnp.bfloat16)).astype(jnp.float32)
    numerator = jnp.einsum('fpq,fqc->fpc', rounded, spatial[..., 2 * HD:])
    spatial_out = (numerator / denominator[..., None]).astype(jnp.bfloat16).reshape(ROWS, HD)
    return jnp.stack([temporal_out, spatial_out], axis=1)

def reference(tokens, modulation, w_qkv, w_out, pattern, counts, spatial_mask):
    hidden = modulate(tokens, modulation)

    def one_pair(weight):
        return pair_attention(hidden, weight, pattern, counts, spatial_mask)
    outputs = lax.map(one_pair, w_qkv.transpose(1, 0, 2))
    attention = outputs.transpose(1, 0, 2, 3).reshape(ROWS, 2 * PAIRS * HD)
    mixed = jnp.dot(attention, w_out, preferred_element_type=jnp.float32)
    return (modulation[2] * mixed).astype(jnp.bfloat16)
```

```python
import functools
import math

import jax
import jax.numpy as jnp
from jax import lax
from jax.experimental import pallas as pl
from jax.experimental.pallas import tpu as pltpu
from jax.sharding import PartitionSpec as P

BLOCK = 128
WIN = 2


EPSILON = 1e-06


def with_halo(cells, sides, width):
    for axis, dim in sides:
        count = lax.axis_size(axis)
        ends = count - 1
        head = lax.slice_in_dim(cells, 0, width, axis=dim)
        tail = lax.slice_in_dim(cells, cells.shape[dim] - width, cells.shape[dim], axis=dim)
        cells = jnp.concatenate(
            [
                lax.ppermute(tail, axis, [(i, (i + 1) % count) for i in range(ends)]),
                cells,
                lax.ppermute(head, axis, [((i + 1) % count, i) for i in range(ends)]),
            ],
            axis=dim,
        )
    return cells


MESH = pl.DeviceIdType.MESH


def pieces_of(rows, most=4):
    for count in range(most, 0, -1):
        if rows % (16 * count) == 0:
            return count
    return 1


class LineGather:
    def __init__(self, own, slots, sems, chunks, count, parts):
        self.own, self.slots, self.chunks = own, slots, chunks
        self.sems, self.count, self.parts = sems, count, parts
        self.me = lax.axis_index("seq")
        self.group = lax.axis_index("groups")
        self.size = own.shape[0] // (parts * chunks)

    def rows(self, group, chunk):
        start = (group * self.chunks + chunk) * self.size
        return pl.ds(pl.multiple_of(start, self.size), self.size)

    def along(self, shard, chunk, way, own):
        rows = self.rows(self.group, chunk)
        source = self.own.at[rows] if own else self.slots.at[shard, rows]
        return pltpu.make_async_remote_copy(
            src_ref=source,
            dst_ref=self.slots.at[shard, rows],
            send_sem=self.sems.at[way, 0, shard, chunk],
            recv_sem=self.sems.at[way, 1, shard, chunk],
            device_id={"seq": self.me + (1 if way == 0 else -1)},
            device_id_type=MESH,
        )

    def across(self, shard, chunk, hop):
        rows = self.rows(self.group, chunk)
        return pltpu.make_async_remote_copy(
            src_ref=self.slots.at[shard, rows],
            dst_ref=self.slots.at[shard, rows],
            send_sem=self.sems.at[1 + hop, 0, shard, chunk],
            recv_sem=self.sems.at[1 + hop, 1, shard, chunk],
            device_id={"groups": lax.rem(self.group + hop, self.parts)},
            device_id_type=MESH,
        )

    def open_line(self):
        for chunk in range(self.chunks):
            for way in (0, 1):
                @pl.when(self.onward(way))
                def _():
                    self.along(self.me, chunk, way, True).start()

    def onward(self, way):
        return self.me < self.count - 1 if way == 0 else self.me > 0

    def shard_of(self, step, way):
        return self.me - step if way == 0 else self.me + step

    def present(self, step, way):
        return self.me >= step if way == 0 else self.me + step < self.count

    def relay(self, step):
        for chunk in range(self.chunks):
            for way in (0, 1):
                shard = self.shard_of(step, way)

                @pl.when(self.present(step, way))
                def _():
                    self.along(shard, chunk, way, False).wait_recv()

                    @pl.when(self.onward(way))
                    def _():
                        self.along(shard, chunk, way, False).start()

                    for hop in range(1, self.parts):
                        self.across(shard, chunk, hop).start()

    def complete(self, shard):
        for chunk in range(self.chunks):
            for hop in range(1, self.parts):
                self.across(shard, chunk, hop).wait_recv()

    def close_sends(self, step):
        for chunk in range(self.chunks):
            for way in (0, 1):
                shard = self.shard_of(step, way)

                @pl.when(self.present(step, way))
                def _():
                    @pl.when(self.onward(way))
                    def _():
                        self.along(shard, chunk, way, False).wait_send()

                    for hop in range(1, self.parts):
                        self.across(shard, chunk, hop).wait_send()

    def close_own(self):
        for chunk in range(self.chunks):
            for way in (0, 1):
                @pl.when(self.onward(way))
                def _():
                    self.along(self.me, chunk, way, True).wait_send()


def project_kernel(count, parts, q_chunks, o_chunks, hidden, w_own, o_own, qkv, o_all, slots, total, q_sems, o_sems, own_sem):
    me = lax.axis_index("seq")
    group = lax.axis_index("groups")
    barrier = pltpu.get_barrier_semaphore()

    @pl.when(me > 0)
    def _():
        pl.semaphore_signal(barrier, inc=1, device_id={"seq": me - 1}, device_id_type=MESH)

    @pl.when(me < count - 1)
    def _():
        pl.semaphore_signal(barrier, inc=1, device_id={"seq": me + 1}, device_id_type=MESH)

    for hop in range(1, parts):
        pl.semaphore_signal(
            barrier, inc=1, device_id={"groups": lax.rem(group + hop, parts)}, device_id_type=MESH
        )
    neighbours = jnp.where(me > 0, 1, 0) + jnp.where(me < count - 1, 1, 0) + (parts - 1)
    pl.semaphore_wait(barrier, neighbours)

    line = LineGather(w_own, slots, q_sems, q_chunks, count, parts)
    outs = LineGather(o_own, o_all, o_sems, o_chunks, count, parts)
    line.open_line()
    keep = pltpu.make_async_copy(o_own, o_all.at[me], own_sem)
    keep.start()
    tile = 256

    def add(shard, block, first):
        def column(j, carry):
            at = pl.ds(pl.multiple_of(j * tile, tile), tile)
            product = jnp.dot(hidden[shard], block[:, at], preferred_element_type=jnp.float32)
            total[:, at] = product if first else total[:, at] + product
            return carry

        lax.fori_loop(0, total.shape[1] // tile, column, 0)

    def finish(step):
        for way in (0, 1):
            shard = line.shard_of(step, way)

            @pl.when(line.present(step, way))
            def _():
                line.complete(shard)
                add(shard, slots.at[shard], False)

    add(me, w_own, True)

    def q_step(step, carry):
        line.relay(step)

        @pl.when(step > 1)
        def _():
            finish(step - 1)

        return carry

    lax.fori_loop(1, count, q_step, 0)
    outs.open_line()
    finish(count - 1)
    qkv[...] = total[...].astype(qkv.dtype)

    def o_step(step, carry):
        outs.relay(step)
        return carry

    lax.fori_loop(1, count, o_step, 0)

    def last(step, carry):
        line.close_sends(step)
        outs.close_sends(step)
        for way in (0, 1):
            shard = outs.shard_of(step, way)

            @pl.when(outs.present(step, way))
            def _():
                outs.complete(shard)

        return carry

    lax.fori_loop(1, count, last, 0)
    line.close_own()
    outs.close_own()
    keep.wait()


def project(hidden, w_own, o_own):
    count, parts = lax.axis_size("seq"), lax.axis_size("groups")
    rows, depth = hidden.shape
    hidden = hidden.reshape(rows, count, depth // count).transpose(1, 0, 2)
    width = w_own.shape[1]
    most = 4 if count <= 8 else 1
    q_chunks = pieces_of(w_own.shape[0] // parts, most)
    o_chunks = pieces_of(o_own.shape[0] // parts, most)
    vmem = pl.BlockSpec(memory_space=pltpu.VMEM)
    return pl.pallas_call(
        functools.partial(project_kernel, count, parts, q_chunks, o_chunks),
        out_shape=[
            jax.ShapeDtypeStruct((rows, width), jnp.bfloat16),
            jax.ShapeDtypeStruct((count,) + o_own.shape, jnp.bfloat16),
        ],
        in_specs=[vmem] * 3,
        out_specs=[vmem, pl.BlockSpec(memory_space=pl.ANY)],
        scratch_shapes=[
            pltpu.VMEM((count,) + w_own.shape, jnp.bfloat16),
            pltpu.VMEM((rows, width), jnp.float32),
            pltpu.SemaphoreType.DMA((1 + parts, 2, count, q_chunks)),
            pltpu.SemaphoreType.DMA((1 + parts, 2, count, o_chunks)),
            pltpu.SemaphoreType.DMA,
        ],
        compiler_params=pltpu.CompilerParams(
            collective_id=0, has_side_effects=True, vmem_limit_bytes=48 * 1024 * 1024
        ),
        name="project",
    )(hidden, w_own, o_own)


def mix_kernel(heads, subs, chunks, attn, w_all, gate, update, slots, total, x_sems, c_sems):
    head, sub = lax.axis_index("head"), lax.axis_index("sub")
    barrier = pltpu.get_barrier_semaphore()
    for hop in range(1, heads):
        pl.semaphore_signal(
            barrier, inc=1, device_id={"head": lax.rem(head + hop, heads)}, device_id_type=MESH
        )
    for hop in range(1, subs):
        pl.semaphore_signal(
            barrier, inc=1, device_id={"sub": lax.rem(sub + hop, subs)}, device_id_type=MESH
        )
    pl.semaphore_wait(barrier, heads + subs - 2)
    size = attn.shape[0] // chunks

    def to_head(hop, chunk):
        rows = pl.ds(chunk * size, size)
        return pltpu.make_async_remote_copy(
            src_ref=attn.at[rows],
            dst_ref=slots.at[hop, 0, rows],
            send_sem=x_sems.at[hop, 0, chunk],
            recv_sem=x_sems.at[hop, 1, chunk],
            device_id={"head": lax.rem(head + hop, heads)},
            device_id_type=MESH,
        )

    def to_sub(hop, turn, chunk):
        rows = pl.ds(chunk * size, size)
        return pltpu.make_async_remote_copy(
            src_ref=attn.at[rows] if hop == 0 else slots.at[hop, 0, rows],
            dst_ref=slots.at[hop, turn, rows],
            send_sem=c_sems.at[hop, turn, 0, chunk],
            recv_sem=c_sems.at[hop, turn, 1, chunk],
            device_id={"sub": lax.rem(sub + turn, subs)},
            device_id_type=MESH,
        )

    for chunk in range(chunks):
        for hop in range(1, heads):
            to_head(hop, chunk).start()
        for turn in range(1, subs):
            to_sub(0, turn, chunk).start()

    def add(chunk, hop, turn, first):
        rows = slice(chunk * size, (chunk + 1) * size)
        owner = lax.rem(head + heads - hop, heads) * subs + lax.rem(sub + subs - turn, subs)
        block = attn[rows, :] if hop == 0 and turn == 0 else slots[hop, turn, rows, :]
        product = jnp.dot(block, w_all[owner], preferred_element_type=jnp.float32)
        total[rows, :] = product if first else total[rows, :] + product

    for chunk in range(chunks):
        add(chunk, 0, 0, True)
    for chunk in range(chunks):
        for turn in range(1, subs):
            to_sub(0, turn, chunk).wait_recv()
            add(chunk, 0, turn, False)
    for chunk in range(chunks):
        for hop in range(1, heads):
            to_head(hop, chunk).wait_recv()
            for turn in range(1, subs):
                to_sub(hop, turn, chunk).start()
            add(chunk, hop, 0, False)
    for chunk in range(chunks):
        for hop in range(1, heads):
            for turn in range(1, subs):
                to_sub(hop, turn, chunk).wait_recv()
                add(chunk, hop, turn, False)
        rows = slice(chunk * size, (chunk + 1) * size)
        update[rows, :] = (gate[...] * total[rows, :]).astype(update.dtype)
    for chunk in range(chunks):
        for hop in range(1, heads):
            to_head(hop, chunk).wait_send()
        for hop in range(heads):
            for turn in range(1, subs):
                to_sub(hop, turn, chunk).wait_send()


def mix(attention, w_all, gate):
    heads, subs = lax.axis_size("head"), lax.axis_size("sub")
    rows, width = attention.shape
    chunks = pieces_of(rows, 2)
    vmem = pl.BlockSpec(memory_space=pltpu.VMEM)
    return pl.pallas_call(
        functools.partial(mix_kernel, heads, subs, chunks),
        out_shape=jax.ShapeDtypeStruct((rows, w_all.shape[-1]), jnp.bfloat16),
        in_specs=[vmem] * 3,
        out_specs=vmem,
        scratch_shapes=[
            pltpu.VMEM((heads, subs, rows, width), jnp.bfloat16),
            pltpu.VMEM((rows, w_all.shape[-1]), jnp.float32),
            pltpu.SemaphoreType.DMA((heads, 2, chunks)),
            pltpu.SemaphoreType.DMA((heads, subs, 2, chunks)),
        ],
        compiler_params=pltpu.CompilerParams(
            collective_id=1, has_side_effects=True, vmem_limit_bytes=40 * 1024 * 1024
        ),
        name="mix",
    )(attention, w_all, gate)


def modulate(tokens, modulation):
    values = tokens.astype(jnp.float32)
    center = jnp.mean(values, axis=-1, keepdims=True)
    spread = jnp.mean(jnp.square(values - center), axis=-1, keepdims=True)
    normed = (values - center) * lax.rsqrt(spread + EPSILON)
    return (normed * (1.0 + modulation[1]) + modulation[0]).astype(jnp.bfloat16)


def shards(tokens, modulation, w_qkv, w_out, pattern, counts, spatial_mask):
    row_count, feature_width = tokens.shape
    pairs_local = w_qkv.shape[1]
    head_size = w_qkv.shape[2] // 6
    frames_local = spatial_mask.shape[0]
    positions = row_count // frames_local
    slot_total = pattern.shape[1]
    scale_factor = 1.0 / math.sqrt(head_size)
    hidden = modulate(tokens, modulation)
    projected, whole_out = project(hidden, w_qkv.reshape(w_qkv.shape[0], -1), w_out)
    packed = projected.reshape(
        frames_local, positions, pairs_local, 6 * head_size
    )
    temporal_in = packed[..., : 3 * head_size].transpose(1, 0, 2, 3)
    received = lax.all_to_all(temporal_in, "seq", split_axis=0, concat_axis=1, tiled=True)
    position_span, frame_total, items, _ = received.shape
    relaid = received.reshape(position_span * frame_total, items, 3 * head_size)
    extended = with_halo(relaid[:, :, head_size:], (("seq", 0),), WIN * BLOCK)
    block_count = position_span * frame_total // BLOCK
    key_table = extended.reshape(block_count + 2 * WIN, BLOCK, items, 2 * head_size)
    queries = relaid[:, :, :head_size].reshape(block_count, BLOCK, items, head_size)
    offsets = pattern - (lax.axis_index("seq") * block_count - WIN)

    def slot_step(slot_index, state_pair):
        numerator, denominator = state_pair
        chosen = lax.dynamic_index_in_dim(offsets, slot_index, 1, keepdims=False)
        picked = jnp.take(key_table, chosen, axis=0)
        scores = (
            jnp.einsum(
                "bqnc,bknc->bnqk",
                queries,
                picked[..., :head_size],
                preferred_element_type=jnp.float32,
            )
            * scale_factor
        )
        alive = (slot_index < counts).astype(jnp.float32)
        weights = jnp.exp(scores) * alive[:, None, None, None]
        numerator = numerator + jnp.einsum(
            "bnqk,bknc->bnqc",
            weights.astype(jnp.bfloat16),
            picked[..., head_size:],
            preferred_element_type=jnp.float32,
        )
        return (numerator, denominator + jnp.sum(weights, axis=-1))

    start_state = (
        jnp.zeros((block_count, items, BLOCK, head_size), jnp.float32),
        jnp.zeros((block_count, items, BLOCK), jnp.float32),
    )
    numerator, denominator = lax.fori_loop(0, slot_total, slot_step, start_state)
    outcome = (numerator / denominator[..., None]).astype(jnp.bfloat16)
    outcome = outcome.transpose(0, 2, 1, 3).reshape(position_span, frame_total, items, head_size)
    temporal_out = lax.all_to_all(outcome, "seq", split_axis=1, concat_axis=0, tiled=True)
    spatial = packed[..., 3 * head_size :]
    blocks_frame = positions // BLOCK
    scores = (
        jnp.einsum(
            "fpnc,fqnc->fnpq",
            spatial[..., :head_size],
            spatial[..., head_size : 2 * head_size],
            preferred_element_type=jnp.float32,
        )
        * scale_factor
    )
    keep = spatial_mask.astype(jnp.float32)[:, None, :, None, :, None]
    weights = (
        jnp.exp(scores).reshape(frames_local, pairs_local, blocks_frame, BLOCK, blocks_frame, BLOCK)
        * keep
    )
    weights = weights.reshape(frames_local, pairs_local, positions, positions)
    denominator = jnp.sum(weights, axis=-1)
    numerator = jnp.einsum(
        "fnpq,fqnc->fpnc",
        weights.astype(jnp.bfloat16),
        spatial[..., 2 * head_size :],
        preferred_element_type=jnp.float32,
    )
    spatial_out = (numerator / denominator.transpose(0, 2, 1)[..., None]).astype(jnp.bfloat16)
    attention = jnp.concatenate([temporal_out.transpose(1, 0, 2, 3), spatial_out], axis=-1)
    attention = attention.reshape(row_count, pairs_local * 2 * head_size)
    out_width = w_out.shape[1]
    blocks = lax.axis_size("head") * lax.axis_size("sub")
    gate_slice = lax.dynamic_slice_in_dim(
        modulation[2], lax.axis_index(("head", "sub")) * out_width, out_width, 0
    )
    return mix(attention, whole_out.reshape(blocks, -1, out_width), gate_slice[None, :])


def solution(mesh):
    return jax.shard_map(
        shards,
        mesh=mesh,
        in_specs=(
            P(("groups", "seq"), None),
            P(),
            P("seq", ("head", "sub"), None),
            P("seq", ("head", "sub")),
            P(("groups", "seq"), None),
            P(("groups", "seq")),
            P(("groups", "seq"), None, None),
        ),
        out_specs=P(("groups", "seq"), ("head", "sub")),
        check_vma=False,
    )
```

```python
import functools
import math

import jax
import jax.numpy as jnp
from jax import lax
from jax.experimental import pallas as pl
from jax.experimental.pallas import tpu as pltpu
from jax.sharding import PartitionSpec as P

BLOCK = 128
WIN = 2


EPSILON = 1e-06


def with_halo(cells, sides, width):
    for axis, dim in sides:
        count = lax.axis_size(axis)
        ends = count - 1
        head = lax.slice_in_dim(cells, 0, width, axis=dim)
        tail = lax.slice_in_dim(cells, cells.shape[dim] - width, cells.shape[dim], axis=dim)
        cells = jnp.concatenate(
            [
                lax.ppermute(tail, axis, [(i, (i + 1) % count) for i in range(ends)]),
                cells,
                lax.ppermute(head, axis, [((i + 1) % count, i) for i in range(ends)]),
            ],
            axis=dim,
        )
    return cells


MESH = pl.DeviceIdType.MESH


def pieces_of(rows, most=4):
    for count in range(most, 0, -1):
        if rows % (16 * count) == 0:
            return count
    return 1


class LineGather:
    def __init__(self, own, slots, sems, chunks, count, parts):
        self.own, self.slots, self.chunks = own, slots, chunks
        self.sems, self.count, self.parts = sems, count, parts
        self.me = lax.axis_index("seq")
        self.group = lax.axis_index("groups")
        self.size = own.shape[0] // (parts * chunks)

    def rows(self, group, chunk):
        start = (group * self.chunks + chunk) * self.size
        return pl.ds(pl.multiple_of(start, self.size), self.size)

    def along(self, shard, chunk, way, own):
        rows = self.rows(self.group, chunk)
        source = self.own.at[rows] if own else self.slots.at[shard, rows]
        return pltpu.make_async_remote_copy(
            src_ref=source,
            dst_ref=self.slots.at[shard, rows],
            send_sem=self.sems.at[way, 0, shard, chunk],
            recv_sem=self.sems.at[way, 1, shard, chunk],
            device_id={"seq": self.me + (1 if way == 0 else -1)},
            device_id_type=MESH,
        )

    def across(self, shard, chunk, hop):
        rows = self.rows(self.group, chunk)
        return pltpu.make_async_remote_copy(
            src_ref=self.slots.at[shard, rows],
            dst_ref=self.slots.at[shard, rows],
            send_sem=self.sems.at[1 + hop, 0, shard, chunk],
            recv_sem=self.sems.at[1 + hop, 1, shard, chunk],
            device_id={"groups": lax.rem(self.group + hop, self.parts)},
            device_id_type=MESH,
        )

    def open_line(self):
        for chunk in range(self.chunks):
            for way in (0, 1):
                @pl.when(self.onward(way))
                def _():
                    self.along(self.me, chunk, way, True).start()

    def onward(self, way):
        return self.me < self.count - 1 if way == 0 else self.me > 0

    def shard_of(self, step, way):
        return self.me - step if way == 0 else self.me + step

    def present(self, step, way):
        return self.me >= step if way == 0 else self.me + step < self.count

    def relay(self, step):
        for chunk in range(self.chunks):
            for way in (0, 1):
                shard = self.shard_of(step, way)

                @pl.when(self.present(step, way))
                def _():
                    self.along(shard, chunk, way, False).wait_recv()

                    @pl.when(self.onward(way))
                    def _():
                        self.along(shard, chunk, way, False).start()

                    for hop in range(1, self.parts):
                        self.across(shard, chunk, hop).start()

    def complete(self, shard):
        for chunk in range(self.chunks):
            for hop in range(1, self.parts):
                self.across(shard, chunk, hop).wait_recv()

    def close_sends(self, step):
        for chunk in range(self.chunks):
            for way in (0, 1):
                shard = self.shard_of(step, way)

                @pl.when(self.present(step, way))
                def _():
                    @pl.when(self.onward(way))
                    def _():
                        self.along(shard, chunk, way, False).wait_send()

                    for hop in range(1, self.parts):
                        self.across(shard, chunk, hop).wait_send()

    def close_own(self):
        for chunk in range(self.chunks):
            for way in (0, 1):
                @pl.when(self.onward(way))
                def _():
                    self.along(self.me, chunk, way, True).wait_send()


def project_kernel(count, parts, q_chunks, o_chunks, hidden, w_own, o_own, qkv, o_all, slots, total, q_sems, o_sems, own_sem):
    me = lax.axis_index("seq")
    group = lax.axis_index("groups")
    barrier = pltpu.get_barrier_semaphore()

    @pl.when(me > 0)
    def _():
        pl.semaphore_signal(barrier, inc=1, device_id={"seq": me - 1}, device_id_type=MESH)

    @pl.when(me < count - 1)
    def _():
        pl.semaphore_signal(barrier, inc=1, device_id={"seq": me + 1}, device_id_type=MESH)

    for hop in range(1, parts):
        pl.semaphore_signal(
            barrier, inc=1, device_id={"groups": lax.rem(group + hop, parts)}, device_id_type=MESH
        )
    neighbours = jnp.where(me > 0, 1, 0) + jnp.where(me < count - 1, 1, 0) + (parts - 1)
    pl.semaphore_wait(barrier, neighbours)

    line = LineGather(w_own, slots, q_sems, q_chunks, count, parts)
    outs = LineGather(o_own, o_all, o_sems, o_chunks, count, parts)
    line.open_line()
    keep = pltpu.make_async_copy(o_own, o_all.at[me], own_sem)
    keep.start()
    tile = 256

    def add(shard, block, first):
        def column(j, carry):
            at = pl.ds(pl.multiple_of(j * tile, tile), tile)
            product = jnp.dot(hidden[shard], block[:, at], preferred_element_type=jnp.float32)
            total[:, at] = product if first else total[:, at] + product
            return carry

        lax.fori_loop(0, total.shape[1] // tile, column, 0)

    def finish(step):
        for way in (0, 1):
            shard = line.shard_of(step, way)

            @pl.when(line.present(step, way))
            def _():
                line.complete(shard)
                add(shard, slots.at[shard], False)

    add(me, w_own, True)

    def q_step(step, carry):
        line.relay(step)

        @pl.when(step > 1)
        def _():
            finish(step - 1)

        return carry

    lax.fori_loop(1, count, q_step, 0)
    outs.open_line()
    finish(count - 1)
    qkv[...] = total[...].astype(qkv.dtype)

    def o_step(step, carry):
        outs.relay(step)
        return carry

    lax.fori_loop(1, count, o_step, 0)

    def last(step, carry):
        line.close_sends(step)
        outs.close_sends(step)
        for way in (0, 1):
            shard = outs.shard_of(step, way)

            @pl.when(outs.present(step, way))
            def _():
                outs.complete(shard)

        return carry

    lax.fori_loop(1, count, last, 0)
    line.close_own()
    outs.close_own()
    keep.wait()


def project(hidden, w_own, o_own):
    count, parts = lax.axis_size("seq"), lax.axis_size("groups")
    rows, depth = hidden.shape
    hidden = hidden.reshape(rows, count, depth // count).transpose(1, 0, 2)
    width = w_own.shape[1]
    most = 4 if count <= 8 else 1
    q_chunks = pieces_of(w_own.shape[0] // parts, most)
    o_chunks = pieces_of(o_own.shape[0] // parts, most)
    vmem = pl.BlockSpec(memory_space=pltpu.VMEM)
    return pl.pallas_call(
        functools.partial(project_kernel, count, parts, q_chunks, o_chunks),
        out_shape=[
            jax.ShapeDtypeStruct((rows, width), jnp.bfloat16),
            jax.ShapeDtypeStruct((count,) + o_own.shape, jnp.bfloat16),
        ],
        in_specs=[vmem] * 3,
        out_specs=[vmem, pl.BlockSpec(memory_space=pl.ANY)],
        scratch_shapes=[
            pltpu.VMEM((count,) + w_own.shape, jnp.bfloat16),
            pltpu.VMEM((rows, width), jnp.float32),
            pltpu.SemaphoreType.DMA((1 + parts, 2, count, q_chunks)),
            pltpu.SemaphoreType.DMA((1 + parts, 2, count, o_chunks)),
            pltpu.SemaphoreType.DMA,
        ],
        compiler_params=pltpu.CompilerParams(
            collective_id=0, has_side_effects=True, vmem_limit_bytes=48 * 1024 * 1024
        ),
        name="project",
    )(hidden, w_own, o_own)


def mix_kernel(heads, subs, chunks, attn, w_all, gate, update, slots, total, x_sems, c_sems):
    head, sub = lax.axis_index("head"), lax.axis_index("sub")
    barrier = pltpu.get_barrier_semaphore()
    for hop in range(1, heads):
        pl.semaphore_signal(
            barrier, inc=1, device_id={"head": lax.rem(head + hop, heads)}, device_id_type=MESH
        )
    for hop in range(1, subs):
        pl.semaphore_signal(
            barrier, inc=1, device_id={"sub": lax.rem(sub + hop, subs)}, device_id_type=MESH
        )
    pl.semaphore_wait(barrier, heads + subs - 2)
    size = attn.shape[0] // chunks

    def to_head(hop, chunk):
        rows = pl.ds(chunk * size, size)
        return pltpu.make_async_remote_copy(
            src_ref=attn.at[rows],
            dst_ref=slots.at[hop, 0, rows],
            send_sem=x_sems.at[hop, 0, chunk],
            recv_sem=x_sems.at[hop, 1, chunk],
            device_id={"head": lax.rem(head + hop, heads)},
            device_id_type=MESH,
        )

    def to_sub(hop, turn, chunk):
        rows = pl.ds(chunk * size, size)
        return pltpu.make_async_remote_copy(
            src_ref=attn.at[rows] if hop == 0 else slots.at[hop, 0, rows],
            dst_ref=slots.at[hop, turn, rows],
            send_sem=c_sems.at[hop, turn, 0, chunk],
            recv_sem=c_sems.at[hop, turn, 1, chunk],
            device_id={"sub": lax.rem(sub + turn, subs)},
            device_id_type=MESH,
        )

    for chunk in range(chunks):
        for hop in range(1, heads):
            to_head(hop, chunk).start()
        for turn in range(1, subs):
            to_sub(0, turn, chunk).start()

    def add(chunk, hop, turn, first):
        rows = slice(chunk * size, (chunk + 1) * size)
        owner = lax.rem(head + heads - hop, heads) * subs + lax.rem(sub + subs - turn, subs)
        block = attn[rows, :] if hop == 0 and turn == 0 else slots[hop, turn, rows, :]
        product = jnp.dot(block, w_all[owner], preferred_element_type=jnp.float32)
        total[rows, :] = product if first else total[rows, :] + product

    for chunk in range(chunks):
        add(chunk, 0, 0, True)
    for chunk in range(chunks):
        for turn in range(1, subs):
            to_sub(0, turn, chunk).wait_recv()
            add(chunk, 0, turn, False)
    for chunk in range(chunks):
        for hop in range(1, heads):
            to_head(hop, chunk).wait_recv()
            for turn in range(1, subs):
                to_sub(hop, turn, chunk).start()
            add(chunk, hop, 0, False)
    for chunk in range(chunks):
        for hop in range(1, heads):
            for turn in range(1, subs):
                to_sub(hop, turn, chunk).wait_recv()
                add(chunk, hop, turn, False)
        rows = slice(chunk * size, (chunk + 1) * size)
        update[rows, :] = (gate[...] * total[rows, :]).astype(update.dtype)
    for chunk in range(chunks):
        for hop in range(1, heads):
            to_head(hop, chunk).wait_send()
        for hop in range(heads):
            for turn in range(1, subs):
                to_sub(hop, turn, chunk).wait_send()


def mix(attention, w_all, gate):
    heads, subs = lax.axis_size("head"), lax.axis_size("sub")
    rows, width = attention.shape
    chunks = pieces_of(rows, 2)
    vmem = pl.BlockSpec(memory_space=pltpu.VMEM)
    return pl.pallas_call(
        functools.partial(mix_kernel, heads, subs, chunks),
        out_shape=jax.ShapeDtypeStruct((rows, w_all.shape[-1]), jnp.bfloat16),
        in_specs=[vmem] * 3,
        out_specs=vmem,
        scratch_shapes=[
            pltpu.VMEM((heads, subs, rows, width), jnp.bfloat16),
            pltpu.VMEM((rows, w_all.shape[-1]), jnp.float32),
            pltpu.SemaphoreType.DMA((heads, 2, chunks)),
            pltpu.SemaphoreType.DMA((heads, subs, 2, chunks)),
        ],
        compiler_params=pltpu.CompilerParams(
            collective_id=1, has_side_effects=True, vmem_limit_bytes=40 * 1024 * 1024
        ),
        name="mix",
    )(attention, w_all, gate)


def modulate(tokens, modulation):
    values = tokens.astype(jnp.float32)
    center = jnp.mean(values, axis=-1, keepdims=True)
    spread = jnp.mean(jnp.square(values - center), axis=-1, keepdims=True)
    normed = (values - center) * lax.rsqrt(spread + EPSILON)
    return (normed * (1.0 + modulation[1]) + modulation[0]).astype(jnp.bfloat16)


def shards(tokens, modulation, w_qkv, w_out, pattern, counts, spatial_mask):
    row_count, feature_width = tokens.shape
    pairs_local = w_qkv.shape[1]
    head_size = w_qkv.shape[2] // 6
    frames_local = spatial_mask.shape[0]
    positions = row_count // frames_local
    slot_total = pattern.shape[1]
    scale_factor = 1.0 / math.sqrt(head_size)
    hidden = modulate(tokens, modulation)
    projected, whole_out = project(hidden, w_qkv.reshape(w_qkv.shape[0], -1), w_out)
    packed = projected.reshape(
        frames_local, positions, pairs_local, 6 * head_size
    )
    temporal_in = packed[..., : 3 * head_size].transpose(1, 0, 2, 3)
    received = lax.all_to_all(temporal_in, "seq", split_axis=0, concat_axis=1, tiled=True)
    position_span, frame_total, items, _ = received.shape
    relaid = received.reshape(position_span * frame_total, items, 3 * head_size)
    extended = with_halo(relaid[:, :, head_size:], (("seq", 0),), WIN * BLOCK)
    block_count = position_span * frame_total // BLOCK
    key_table = extended.reshape(block_count + 2 * WIN, BLOCK, items, 2 * head_size)
    queries = relaid[:, :, :head_size].reshape(block_count, BLOCK, items, head_size)
    offsets = pattern - (lax.axis_index("seq") * block_count - WIN)

    def slot_step(slot_index, state_pair):
        numerator, denominator = state_pair
        chosen = lax.dynamic_index_in_dim(offsets, slot_index, 1, keepdims=False)
        picked = jnp.take(key_table, chosen, axis=0)
        scores = (
            jnp.einsum(
                "bqnc,bknc->bnqk",
                queries,
                picked[..., :head_size],
                preferred_element_type=jnp.float32,
            )
            * scale_factor
        )
        alive = (slot_index < counts).astype(jnp.float32)
        weights = jnp.exp(scores) * alive[:, None, None, None]
        numerator = numerator + jnp.einsum(
            "bnqk,bknc->bnqc",
            weights.astype(jnp.bfloat16),
            picked[..., head_size:],
            preferred_element_type=jnp.float32,
        )
        return (numerator, denominator + jnp.sum(weights, axis=-1))

    start_state = (
        jnp.zeros((block_count, items, BLOCK, head_size), jnp.float32),
        jnp.zeros((block_count, items, BLOCK), jnp.float32),
    )
    numerator, denominator = lax.fori_loop(0, slot_total, slot_step, start_state)
    outcome = (numerator / denominator[..., None]).astype(jnp.bfloat16)
    outcome = outcome.transpose(0, 2, 1, 3).reshape(position_span, frame_total, items, head_size)
    temporal_out = lax.all_to_all(outcome, "seq", split_axis=1, concat_axis=0, tiled=True)
    spatial = packed[..., 3 * head_size :]
    blocks_frame = positions // BLOCK
    scores = (
        jnp.einsum(
            "fpnc,fqnc->fnpq",
            spatial[..., :head_size],
            spatial[..., head_size : 2 * head_size],
            preferred_element_type=jnp.float32,
        )
        * scale_factor
    )
    keep = spatial_mask.astype(jnp.float32)[:, None, :, None, :, None]
    weights = (
        jnp.exp(scores).reshape(frames_local, pairs_local, blocks_frame, BLOCK, blocks_frame, BLOCK)
        * keep
    )
    weights = weights.reshape(frames_local, pairs_local, positions, positions)
    denominator = jnp.sum(weights, axis=-1)
    numerator = jnp.einsum(
        "fnpq,fqnc->fpnc",
        weights.astype(jnp.bfloat16),
        spatial[..., 2 * head_size :],
        preferred_element_type=jnp.float32,
    )
    spatial_out = (numerator / denominator.transpose(0, 2, 1)[..., None]).astype(jnp.bfloat16)
    attention = jnp.concatenate([temporal_out.transpose(1, 0, 2, 3), spatial_out], axis=-1)
    attention = attention.reshape(row_count, pairs_local * 2 * head_size)
    out_width = w_out.shape[1]
    blocks = lax.axis_size("head") * lax.axis_size("sub")
    gate_slice = lax.dynamic_slice_in_dim(
        modulation[2], lax.axis_index(("head", "sub")) * out_width, out_width, 0
    )
    return mix(attention, whole_out.reshape(blocks, -1, out_width), gate_slice[None, :])

def meet(axes):
    barrier = pltpu.get_barrier_semaphore()
    others = 0
    for axis in axes:
        size = lax.axis_size(axis)
        for hop in range(1, size):
            other = lax.rem(lax.axis_index(axis) + hop, size)
            pl.semaphore_signal(barrier, inc=1, device_id={axis: other}, device_id_type=MESH)
            others += 1
    pl.semaphore_wait(barrier, others)


def push(source, target, send_sem, recv_sem, axis, place):
    return pltpu.make_async_remote_copy(
        src_ref=source,
        dst_ref=target,
        send_sem=send_sem,
        recv_sem=recv_sem,
        device_id={axis: place},
        device_id_type=MESH,
    )


def by_head_kernel(
    sizes, chunks, o_chunks, span, hid_own, w_parts, o_own, lists, blocks, o_all, lists_all,
    hfull, wfull, w_sems, l_sems, z_sems, x_sems, c_sems, o_sems, own_sems,
):
    count, parts, heads, subs = sizes
    me, group = lax.axis_index("seq"), lax.axis_index("groups")
    head, sub = lax.axis_index("head"), lax.axis_index("sub")
    meet(("seq", "groups", "head", "sub"))
    quarter = hid_own.shape[0]
    size = quarter // chunks
    half = w_parts.shape[1] // parts
    mine = pl.ds(pl.multiple_of(group * half, half), half)

    def place(hop, axis, size_):
        return lax.rem(lax.axis_index(axis) + hop, size_)

    def source_of(hop):
        return lax.rem(me + count - hop, count)

    def w_along(hop, shard):
        return push(
            w_parts.at[place(hop, "seq", count), mine], wfull.at[shard, mine],
            w_sems.at[0, 0, hop], w_sems.at[0, 1, hop], "seq", place(hop, "seq", count),
        )

    def w_across(hop, turn):
        spot = wfull.at[source_of(hop), mine]
        return push(
            spot, spot, w_sems.at[turn, 0, hop], w_sems.at[turn, 1, hop],
            "groups", place(turn, "groups", parts),
        )

    def l_along(hop):
        return push(
            lists, lists_all.at[me], l_sems.at[0, hop], l_sems.at[1, hop],
            "seq", place(hop, "seq", count),
        )

    def rows_of(head_hop, sub_hop, chunk):
        owner = lax.rem(head + heads - head_hop, heads) * subs + lax.rem(sub + subs - sub_hop, subs)
        return pl.ds(pl.multiple_of(owner * quarter + chunk * size, size), size)

    def spot(shard, head_hop, sub_hop, chunk):
        return hfull.at[shard, rows_of(head_hop, sub_hop, chunk)]

    def z_push(shard, chunk, way, own):
        target = spot(shard, 0, 0, chunk)
        return push(
            hid_own.at[pl.ds(chunk * size, size)] if own else target, target,
            z_sems.at[way, 0, shard, chunk], z_sems.at[way, 1, shard, chunk],
            "seq", me + (1 if way == 0 else -1),
        )

    def x_push(shard, chunk, hop, own=False):
        target = spot(shard, 0, 0, chunk)
        return push(
            hid_own.at[pl.ds(chunk * size, size)] if own else target, target,
            x_sems.at[hop, 0, shard, chunk], x_sems.at[hop, 1, shard, chunk],
            "head", place(hop, "head", heads),
        )

    def c_push(shard, chunk, hop, turn, own=False):
        target = spot(shard, hop, 0, chunk)
        return push(
            hid_own.at[pl.ds(chunk * size, size)] if own else target, target,
            c_sems.at[hop, turn, 0, shard, chunk], c_sems.at[hop, turn, 1, shard, chunk],
            "sub", place(turn, "sub", subs),
        )

    outs = LineGather(o_own, o_all, o_sems, o_chunks, count, parts)
    onward, shard_of, present = outs.onward, outs.shard_of, outs.present
    ways = lambda step: (0, 1) if step else (0,)

    for hop in range(1, count):
        l_along(hop).start()
    for hop in range(1, count):
        w_along(hop, me).start()
    for chunk in range(chunks):
        for way in (0, 1):
            @pl.when(onward(way))
            def _():
                z_push(me, chunk, way, True).start()
        for hop in range(1, heads):
            x_push(me, chunk, hop, True).start()
        for turn in range(1, subs):
            c_push(me, chunk, 0, turn, True).start()
    keeps = [
        pltpu.make_async_copy(o_own, o_all.at[me], own_sems.at[0]),
        pltpu.make_async_copy(w_parts.at[me], wfull.at[me], own_sems.at[1]),
        pltpu.make_async_copy(
            hid_own,
            hfull.at[me, pl.ds(pl.multiple_of((head * subs + sub) * quarter, quarter), quarter)],
            own_sems.at[2],
        ),
        pltpu.make_async_copy(lists, lists_all.at[me], own_sems.at[3]),
    ]
    for keep in keeps:
        keep.start()

    for hop in range(1, count):
        w_along(hop, source_of(hop)).wait_recv()
        for turn in range(1, parts):
            w_across(hop, turn).start()

    def z_relay(step):
        for chunk in range(chunks):
            for way in ways(step):
                shard = shard_of(step, way)

                @pl.when(present(step, way))
                def _():
                    z_push(shard, chunk, way, False).wait_recv()

                    @pl.when(onward(way))
                    def _():
                        z_push(shard, chunk, way, False).start()

                    for hop in range(1, heads):
                        x_push(shard, chunk, hop).start()
                    for turn in range(1, subs):
                        c_push(shard, chunk, 0, turn).start()

    def x_relay(step):
        for chunk in range(chunks):
            for way in ways(step):
                shard = shard_of(step, way)

                @pl.when(present(step, way))
                def _():
                    for hop in range(1, heads):
                        x_push(shard, chunk, hop).wait_recv()
                        for turn in range(1, subs):
                            c_push(shard, chunk, hop, turn).start()

    def finish(step):
        for way in ways(step):
            shard = shard_of(step, way)

            @pl.when(present(step, way))
            def _():
                for chunk in range(chunks):
                    for hop in range(heads):
                        for turn in range(1, subs):
                            c_push(shard, chunk, hop, turn).wait_recv()
                weight = wfull[...].reshape(-1, wfull.shape[-1])
                total = jnp.dot(hfull[shard], weight, preferred_element_type=jnp.float32)
                total = total.astype(blocks.dtype)
                rows = total.shape[0]

                @pl.when(lax.rem(me, 2) == 0)
                def _():
                    at = pl.ds(pl.multiple_of(shard * span, span), span)
                    for i in range(rows // span):
                        blocks[i, at, :] = total[i * span : (i + 1) * span]

                @pl.when(lax.rem(me, 2) == 1)
                def _():
                    each = blocks.shape[1]
                    for i in range(rows // each):
                        blocks[shard * (rows // each) + i] = total[i * each : (i + 1) * each]

    for step in range(1, count):
        z_relay(step)
        if step == count - 1:
            outs.open_line()
        if step == 2:
            for keep in keeps:
                keep.wait()
            for hop in range(1, count):
                for turn in range(1, parts):
                    w_across(hop, turn).wait_recv()
        if step >= 2:
            x_relay(step - 2)
            finish(step - 2)
    x_relay(count - 2)
    outs.relay(1)
    finish(count - 2)
    x_relay(count - 1)
    finish(count - 1)
    for step in range(2, count):
        outs.relay(step)

    for hop in range(1, count):
        l_along(hop).wait_recv()
        l_along(hop).wait_send()
        w_along(hop, me).wait_send()
        for turn in range(1, parts):
            w_across(hop, turn).wait_send()
    for step in range(count):
        for way in ways(step):
            shard = shard_of(step, way)

            @pl.when(present(step, way))
            def _():
                for chunk in range(chunks):
                    for side in (0, 1) if step == 0 else (way,):
                        @pl.when(onward(side))
                        def _():
                            z_push(shard, chunk, side, False).wait_send()
                    for hop in range(1, heads):
                        x_push(shard, chunk, hop).wait_send()
                    for hop in range(heads):
                        for turn in range(1, subs):
                            c_push(shard, chunk, hop, turn).wait_send()
    for step in range(1, count):
        outs.close_sends(step)
        for way in (0, 1):
            @pl.when(outs.present(step, way))
            def _():
                outs.complete(outs.shard_of(step, way))
    outs.close_own()


def by_head(hid_own, w_parts, o_own, lists, span, block):
    sizes = tuple(lax.axis_size(axis) for axis in ("seq", "groups", "head", "sub"))
    count, parts, heads, subs = sizes
    rows = hid_own.shape[0] * heads * subs
    depth, width = hid_own.shape[1], w_parts.shape[2]
    chunks = pieces_of(hid_own.shape[0], 2)
    o_chunks = pieces_of(o_own.shape[0] // parts, 2)
    vmem = pl.BlockSpec(memory_space=pltpu.VMEM)
    dma = pltpu.SemaphoreType.DMA
    return pl.pallas_call(
        functools.partial(by_head_kernel, sizes, chunks, o_chunks, span),
        out_shape=[
            jax.ShapeDtypeStruct((count * rows // block, block, width), jnp.bfloat16),
            jax.ShapeDtypeStruct((count,) + o_own.shape, jnp.bfloat16),
            jax.ShapeDtypeStruct((count,) + lists.shape, lists.dtype),
        ],
        in_specs=[vmem] * 4,
        out_specs=[vmem, pl.BlockSpec(memory_space=pl.ANY), vmem],
        scratch_shapes=[
            pltpu.VMEM((count, rows, depth), jnp.bfloat16),
            pltpu.VMEM((count,) + w_parts.shape[1:], jnp.bfloat16),
            dma((parts, 2, count)),
            dma((2, count)),
            dma((2, 2, count, chunks)),
            dma((heads, 2, count, chunks)),
            dma((heads, subs, 2, count, chunks)),
            dma((1 + parts, 2, count, o_chunks)),
            dma((4,)),
        ],
        compiler_params=pltpu.CompilerParams(
            collective_id=2, has_side_effects=True, vmem_limit_bytes=48 * 1024 * 1024
        ),
        name="by_head",
    )(hid_own, w_parts, o_own, lists)


def attend_kernel(count, span, scale, role, index, alive, blocks, out):
    total, block, width = blocks.shape
    size = width // 3
    slots = index.shape[1]
    each = total // count

    def query(b, carry):
        q = blocks[b, :, :size]
        numerator = jnp.zeros((block, size), jnp.float32)
        denominator = jnp.zeros((block, 1), jnp.float32)
        for j in range(slots):
            at = index[b, j]
            scores = lax.dot_general(
                q, blocks[at, :, size : 2 * size], (((1,), (1,)), ((), ())),
                preferred_element_type=jnp.float32,
            )
            weights = jnp.exp(scores * scale) * alive[b, j]
            denominator = denominator + jnp.sum(weights, axis=-1, keepdims=True)
            numerator = numerator + jnp.dot(
                weights.astype(jnp.bfloat16), blocks[at, :, 2 * size :],
                preferred_element_type=jnp.float32,
            )
        result = (numerator / denominator).astype(out.dtype)

        @pl.when(role[0] == 0)
        def _():
            at = pl.ds(pl.multiple_of(b * span, span), span)
            for f in range(count):
                out[f, at, :] = result[f * span : (f + 1) * span]

        @pl.when(role[0] == 1)
        def _():
            at = pl.ds(pl.multiple_of(lax.rem(b, each) * block, block), block)
            out[b // each, at, :] = result

        return carry

    lax.fori_loop(0, total, query, 0, unroll=2)


def attend(role, index, alive, blocks, count, span):
    total, block, width = blocks.shape
    size = width // 3
    smem = pl.BlockSpec(memory_space=pltpu.SMEM)
    vmem = pl.BlockSpec(memory_space=pltpu.VMEM)
    return pl.pallas_call(
        functools.partial(attend_kernel, count, span, 1.0 / math.sqrt(size)),
        out_shape=jax.ShapeDtypeStruct((count, total * block // count, size), jnp.bfloat16),
        in_specs=[smem, smem, smem, vmem],
        out_specs=vmem,
        name="attend",
    )(role, index, alive, blocks)


def spread_kernel(
    count, heads, subs, own, w_all, gate, update, slots, total, z_sems, x_sems, c_sems, own_sem
):
    me, head, sub = (lax.axis_index(axis) for axis in ("seq", "head", "sub"))
    meet(("seq", "head", "sub"))
    size = own.shape[2]

    def columns(step):
        source = lax.rem(me + count - step, count)
        return pl.ds(pl.multiple_of(source * size, size), size)

    def spot(hop, turn, step):
        return slots.at[hop, turn, :, columns(step)]

    def to_seq(step):
        other = lax.rem(me + step, count)
        return push(
            own.at[other], spot(0, 0, 0), z_sems.at[0, step], z_sems.at[1, step], "seq", other
        )

    def to_head(hop, step):
        return push(
            own.at[me] if step == 0 else spot(0, 0, step), spot(hop, 0, step),
            x_sems.at[hop, 0, step], x_sems.at[hop, 1, step],
            "head", lax.rem(head + hop, heads),
        )

    def to_sub(hop, turn, step):
        return push(
            own.at[me] if hop == 0 and step == 0 else spot(hop, 0, step), spot(hop, turn, step),
            c_sems.at[hop, turn, 0, step], c_sems.at[hop, turn, 1, step],
            "sub", lax.rem(sub + turn, subs),
        )

    def hand_over(step):
        for hop in range(1, heads):
            to_head(hop, step).start()
        for turn in range(1, subs):
            to_sub(0, turn, step).start()

    def pass_on(step):
        for hop in range(1, heads):
            to_head(hop, step).wait_recv()
            for turn in range(1, subs):
                to_sub(hop, turn, step).start()

    for step in range(1, count):
        to_seq(step).start()
    hand_over(0)
    keep = pltpu.make_async_copy(own.at[me], spot(0, 0, 0), own_sem)
    keep.start()
    for step in range(1, count):
        to_seq(step).wait_recv()
        hand_over(step)
        pass_on(step - 1)
    keep.wait()

    def add(hop, turn, first):
        owner = lax.rem(head + heads - hop, heads) * subs + lax.rem(sub + subs - turn, subs)
        product = jnp.dot(slots[hop, turn], w_all[owner], preferred_element_type=jnp.float32)
        total[...] = product if first else total[...] + product

    add(0, 0, True)
    pass_on(count - 1)
    for hop in range(heads):
        if hop:
            add(hop, 0, False)
        for turn in range(1, subs):
            for step in range(count):
                to_sub(hop, turn, step).wait_recv()
            add(hop, turn, False)
    update[...] = (gate[...] * total[...]).astype(update.dtype)
    for step in range(count):
        if step:
            to_seq(step).wait_send()
        for hop in range(1, heads):
            to_head(hop, step).wait_send()
        for hop in range(heads):
            for turn in range(1, subs):
                to_sub(hop, turn, step).wait_send()


def spread(own, w_all, gate):
    count, heads, subs = (lax.axis_size(axis) for axis in ("seq", "head", "sub"))
    rows, size = own.shape[1:]
    vmem = pl.BlockSpec(memory_space=pltpu.VMEM)
    dma = pltpu.SemaphoreType.DMA
    return pl.pallas_call(
        functools.partial(spread_kernel, count, heads, subs),
        out_shape=jax.ShapeDtypeStruct((rows, w_all.shape[-1]), jnp.bfloat16),
        in_specs=[vmem] * 3,
        out_specs=vmem,
        scratch_shapes=[
            pltpu.VMEM((heads, subs, rows, count * size), jnp.bfloat16),
            pltpu.VMEM((rows, w_all.shape[-1]), jnp.float32),
            dma((2, count)),
            dma((heads, 2, count)),
            dma((heads, subs, 2, count)),
            dma,
        ],
        compiler_params=pltpu.CompilerParams(
            collective_id=3, has_side_effects=True, vmem_limit_bytes=40 * 1024 * 1024
        ),
        name="spread",
    )(own, w_all, gate)


def shards_by_head(tokens, modulation, w_qkv, w_out, pattern, counts, spatial_mask):
    count = lax.axis_size("seq")
    blocks = lax.axis_size("head") * lax.axis_size("sub")
    row_count = tokens.shape[0]
    depth, pairs_local, width = w_qkv.shape
    quarter = row_count // blocks
    place = lax.axis_index(("head", "sub"))
    span = BLOCK // count
    hid_own = modulate(lax.dynamic_slice_in_dim(tokens, place * quarter, quarter, 0), modulation)
    w_parts = w_qkv.reshape(depth, count, width // 2).transpose(1, 0, 2)
    slot_total = pattern.shape[1]
    entries = jnp.concatenate([pattern.reshape(-1), counts.reshape(-1), spatial_mask.reshape(-1)])
    lists = jnp.pad(entries, (0, 8 * 128 - entries.shape[0])).reshape(8, 128)
    heads_in, whole_out, lists_all = by_head(hid_own, w_parts, w_out, lists, span, BLOCK)
    entries = lists_all.reshape(count, -1)
    listed = pattern.shape[0] * slot_total
    table = entries[:, :listed].reshape(-1, slot_total)
    used = entries[:, listed : listed + counts.shape[0]].reshape(-1)
    masked = entries[:, listed + counts.shape[0] :][:, : spatial_mask.size].reshape(-1, slot_total)
    order = jnp.arange(slot_total, dtype=jnp.int32)
    query = jnp.arange(table.shape[0], dtype=jnp.int32)
    frame_blocks = (query // slot_total * slot_total)[:, None] + order[None, :]
    role = lax.rem(lax.axis_index("seq"), 2)
    index = jnp.where(role == 0, table, frame_blocks)
    alive = jnp.where(role == 0, order[None, :] < used[:, None], masked > 0).astype(jnp.float32)
    own = attend(role[None], index, alive, heads_in, count, span)
    out_width = w_out.shape[1]
    gate_slice = lax.dynamic_slice_in_dim(modulation[2], place * out_width, out_width, 0)
    return spread(own, whole_out.reshape(blocks, -1, out_width), gate_slice[None, :])


def one_head_each(mesh_count, blocks, tokens, w_qkv, pattern, spatial_mask):
    rows, frames = tokens.shape[0], spatial_mask.shape[0]
    return (
        w_qkv.shape[1] * 2 == mesh_count > 2
        and frames == 1
        and spatial_mask.shape[2] == pattern.shape[1]
        and rows == BLOCK * spatial_mask.shape[1]
        and BLOCK % (16 * mesh_count) == 0
        and w_qkv.shape[0] % 128 == 0
        and rows % (16 * blocks) == 0
    )


def shards_any(*args):
    tokens, _, w_qkv, _, pattern, _, spatial_mask = args
    blocks = lax.axis_size("head") * lax.axis_size("sub")
    if one_head_each(lax.axis_size("seq"), blocks, tokens, w_qkv, pattern, spatial_mask):
        return shards_by_head(*args)
    return shards(*args)


def solution(mesh):
    return jax.shard_map(
        shards_any,
        mesh=mesh,
        in_specs=(
            P(("groups", "seq"), None),
            P(),
            P("seq", ("head", "sub"), None),
            P("seq", ("head", "sub")),
            P(("groups", "seq"), None),
            P(("groups", "seq")),
            P(("groups", "seq"), None, None),
        ),
        out_specs=P(("groups", "seq"), ("head", "sub")),
        check_vma=False,
    )
```

```python
import functools
import math

import jax
import jax.numpy as jnp
from jax import lax
from jax.experimental import pallas as pl
from jax.experimental.pallas import tpu as pltpu
from jax.sharding import PartitionSpec as P

BLOCK = 128
WIN = 2


EPSILON = 1e-06


def with_halo(cells, sides, width):
    for axis, dim in sides:
        count = lax.axis_size(axis)
        ends = count - 1
        head = lax.slice_in_dim(cells, 0, width, axis=dim)
        tail = lax.slice_in_dim(cells, cells.shape[dim] - width, cells.shape[dim], axis=dim)
        cells = jnp.concatenate(
            [
                lax.ppermute(tail, axis, [(i, (i + 1) % count) for i in range(ends)]),
                cells,
                lax.ppermute(head, axis, [((i + 1) % count, i) for i in range(ends)]),
            ],
            axis=dim,
        )
    return cells


MESH = pl.DeviceIdType.MESH


def pieces_of(rows, most=4):
    for count in range(most, 0, -1):
        if rows % (16 * count) == 0:
            return count
    return 1


class LineGather:
    def __init__(self, own, slots, sems, chunks, count, parts):
        self.own, self.slots, self.chunks = own, slots, chunks
        self.sems, self.count, self.parts = sems, count, parts
        self.me = lax.axis_index("seq")
        self.group = lax.axis_index("groups")
        self.size = own.shape[0] // (parts * chunks)

    def rows(self, group, chunk):
        start = (group * self.chunks + chunk) * self.size
        return pl.ds(pl.multiple_of(start, self.size), self.size)

    def along(self, shard, chunk, way, own):
        rows = self.rows(self.group, chunk)
        source = self.own.at[rows] if own else self.slots.at[shard, rows]
        return pltpu.make_async_remote_copy(
            src_ref=source,
            dst_ref=self.slots.at[shard, rows],
            send_sem=self.sems.at[way, 0, shard, chunk],
            recv_sem=self.sems.at[way, 1, shard, chunk],
            device_id={"seq": self.me + (1 if way == 0 else -1)},
            device_id_type=MESH,
        )

    def across(self, shard, chunk, hop):
        rows = self.rows(self.group, chunk)
        return pltpu.make_async_remote_copy(
            src_ref=self.slots.at[shard, rows],
            dst_ref=self.slots.at[shard, rows],
            send_sem=self.sems.at[1 + hop, 0, shard, chunk],
            recv_sem=self.sems.at[1 + hop, 1, shard, chunk],
            device_id={"groups": lax.rem(self.group + hop, self.parts)},
            device_id_type=MESH,
        )

    def open_line(self):
        for chunk in range(self.chunks):
            for way in (0, 1):
                @pl.when(self.onward(way))
                def _():
                    self.along(self.me, chunk, way, True).start()

    def onward(self, way):
        return self.me < self.count - 1 if way == 0 else self.me > 0

    def shard_of(self, step, way):
        return self.me - step if way == 0 else self.me + step

    def present(self, step, way):
        return self.me >= step if way == 0 else self.me + step < self.count

    def relay(self, step):
        for chunk in range(self.chunks):
            for way in (0, 1):
                shard = self.shard_of(step, way)

                @pl.when(self.present(step, way))
                def _():
                    self.along(shard, chunk, way, False).wait_recv()

                    @pl.when(self.onward(way))
                    def _():
                        self.along(shard, chunk, way, False).start()

                    for hop in range(1, self.parts):
                        self.across(shard, chunk, hop).start()

    def complete(self, shard):
        for chunk in range(self.chunks):
            for hop in range(1, self.parts):
                self.across(shard, chunk, hop).wait_recv()

    def close_sends(self, step):
        for chunk in range(self.chunks):
            for way in (0, 1):
                shard = self.shard_of(step, way)

                @pl.when(self.present(step, way))
                def _():
                    @pl.when(self.onward(way))
                    def _():
                        self.along(shard, chunk, way, False).wait_send()

                    for hop in range(1, self.parts):
                        self.across(shard, chunk, hop).wait_send()

    def close_own(self):
        for chunk in range(self.chunks):
            for way in (0, 1):
                @pl.when(self.onward(way))
                def _():
                    self.along(self.me, chunk, way, True).wait_send()


def project_kernel(count, parts, q_chunks, o_chunks, hidden, w_own, o_own, qkv, o_all, slots, total, q_sems, o_sems, own_sem):
    me = lax.axis_index("seq")
    group = lax.axis_index("groups")
    barrier = pltpu.get_barrier_semaphore()

    @pl.when(me > 0)
    def _():
        pl.semaphore_signal(barrier, inc=1, device_id={"seq": me - 1}, device_id_type=MESH)

    @pl.when(me < count - 1)
    def _():
        pl.semaphore_signal(barrier, inc=1, device_id={"seq": me + 1}, device_id_type=MESH)

    for hop in range(1, parts):
        pl.semaphore_signal(
            barrier, inc=1, device_id={"groups": lax.rem(group + hop, parts)}, device_id_type=MESH
        )
    neighbours = jnp.where(me > 0, 1, 0) + jnp.where(me < count - 1, 1, 0) + (parts - 1)
    pl.semaphore_wait(barrier, neighbours)

    line = LineGather(w_own, slots, q_sems, q_chunks, count, parts)
    outs = LineGather(o_own, o_all, o_sems, o_chunks, count, parts)
    line.open_line()
    keep = pltpu.make_async_copy(o_own, o_all.at[me], own_sem)
    keep.start()
    tile = 256

    def add(shard, block, first):
        def column(j, carry):
            at = pl.ds(pl.multiple_of(j * tile, tile), tile)
            product = jnp.dot(hidden[shard], block[:, at], preferred_element_type=jnp.float32)
            total[:, at] = product if first else total[:, at] + product
            return carry

        lax.fori_loop(0, total.shape[1] // tile, column, 0)

    def finish(step):
        for way in (0, 1):
            shard = line.shard_of(step, way)

            @pl.when(line.present(step, way))
            def _():
                line.complete(shard)
                add(shard, slots.at[shard], False)

    add(me, w_own, True)

    def q_step(step, carry):
        line.relay(step)

        @pl.when(step > 1)
        def _():
            finish(step - 1)

        return carry

    lax.fori_loop(1, count, q_step, 0)
    outs.open_line()
    finish(count - 1)
    qkv[...] = total[...].astype(qkv.dtype)

    def o_step(step, carry):
        outs.relay(step)
        return carry

    lax.fori_loop(1, count, o_step, 0)

    def last(step, carry):
        line.close_sends(step)
        outs.close_sends(step)
        for way in (0, 1):
            shard = outs.shard_of(step, way)

            @pl.when(outs.present(step, way))
            def _():
                outs.complete(shard)

        return carry

    lax.fori_loop(1, count, last, 0)
    line.close_own()
    outs.close_own()
    keep.wait()


def project(hidden, w_own, o_own):
    count, parts = lax.axis_size("seq"), lax.axis_size("groups")
    rows, depth = hidden.shape
    hidden = hidden.reshape(rows, count, depth // count).transpose(1, 0, 2)
    width = w_own.shape[1]
    most = 4 if count <= 8 else 1
    q_chunks = pieces_of(w_own.shape[0] // parts, most)
    o_chunks = pieces_of(o_own.shape[0] // parts, most)
    vmem = pl.BlockSpec(memory_space=pltpu.VMEM)
    return pl.pallas_call(
        functools.partial(project_kernel, count, parts, q_chunks, o_chunks),
        out_shape=[
            jax.ShapeDtypeStruct((rows, width), jnp.bfloat16),
            jax.ShapeDtypeStruct((count,) + o_own.shape, jnp.bfloat16),
        ],
        in_specs=[vmem] * 3,
        out_specs=[vmem, pl.BlockSpec(memory_space=pl.ANY)],
        scratch_shapes=[
            pltpu.VMEM((count,) + w_own.shape, jnp.bfloat16),
            pltpu.VMEM((rows, width), jnp.float32),
            pltpu.SemaphoreType.DMA((1 + parts, 2, count, q_chunks)),
            pltpu.SemaphoreType.DMA((1 + parts, 2, count, o_chunks)),
            pltpu.SemaphoreType.DMA,
        ],
        compiler_params=pltpu.CompilerParams(
            collective_id=0, has_side_effects=True, vmem_limit_bytes=48 * 1024 * 1024
        ),
        name="project",
    )(hidden, w_own, o_own)


def mix_kernel(heads, subs, chunks, attn, w_all, gate, update, slots, total, x_sems, c_sems):
    head, sub = lax.axis_index("head"), lax.axis_index("sub")
    barrier = pltpu.get_barrier_semaphore()
    for hop in range(1, heads):
        pl.semaphore_signal(
            barrier, inc=1, device_id={"head": lax.rem(head + hop, heads)}, device_id_type=MESH
        )
    for hop in range(1, subs):
        pl.semaphore_signal(
            barrier, inc=1, device_id={"sub": lax.rem(sub + hop, subs)}, device_id_type=MESH
        )
    pl.semaphore_wait(barrier, heads + subs - 2)
    size = attn.shape[0] // chunks

    def to_head(hop, chunk):
        rows = pl.ds(chunk * size, size)
        return pltpu.make_async_remote_copy(
            src_ref=attn.at[rows],
            dst_ref=slots.at[hop, 0, rows],
            send_sem=x_sems.at[hop, 0, chunk],
            recv_sem=x_sems.at[hop, 1, chunk],
            device_id={"head": lax.rem(head + hop, heads)},
            device_id_type=MESH,
        )

    def to_sub(hop, turn, chunk):
        rows = pl.ds(chunk * size, size)
        return pltpu.make_async_remote_copy(
            src_ref=attn.at[rows] if hop == 0 else slots.at[hop, 0, rows],
            dst_ref=slots.at[hop, turn, rows],
            send_sem=c_sems.at[hop, turn, 0, chunk],
            recv_sem=c_sems.at[hop, turn, 1, chunk],
            device_id={"sub": lax.rem(sub + turn, subs)},
            device_id_type=MESH,
        )

    for chunk in range(chunks):
        for hop in range(1, heads):
            to_head(hop, chunk).start()
        for turn in range(1, subs):
            to_sub(0, turn, chunk).start()

    def add(chunk, hop, turn, first):
        rows = slice(chunk * size, (chunk + 1) * size)
        owner = lax.rem(head + heads - hop, heads) * subs + lax.rem(sub + subs - turn, subs)
        block = attn[rows, :] if hop == 0 and turn == 0 else slots[hop, turn, rows, :]
        product = jnp.dot(block, w_all[owner], preferred_element_type=jnp.float32)
        total[rows, :] = product if first else total[rows, :] + product

    for chunk in range(chunks):
        add(chunk, 0, 0, True)
    for chunk in range(chunks):
        for turn in range(1, subs):
            to_sub(0, turn, chunk).wait_recv()
            add(chunk, 0, turn, False)
    for chunk in range(chunks):
        for hop in range(1, heads):
            to_head(hop, chunk).wait_recv()
            for turn in range(1, subs):
                to_sub(hop, turn, chunk).start()
            add(chunk, hop, 0, False)
    for chunk in range(chunks):
        for hop in range(1, heads):
            for turn in range(1, subs):
                to_sub(hop, turn, chunk).wait_recv()
                add(chunk, hop, turn, False)
        rows = slice(chunk * size, (chunk + 1) * size)
        update[rows, :] = (gate[...] * total[rows, :]).astype(update.dtype)
    for chunk in range(chunks):
        for hop in range(1, heads):
            to_head(hop, chunk).wait_send()
        for hop in range(heads):
            for turn in range(1, subs):
                to_sub(hop, turn, chunk).wait_send()


def mix(attention, w_all, gate):
    heads, subs = lax.axis_size("head"), lax.axis_size("sub")
    rows, width = attention.shape
    chunks = pieces_of(rows, 2)
    vmem = pl.BlockSpec(memory_space=pltpu.VMEM)
    return pl.pallas_call(
        functools.partial(mix_kernel, heads, subs, chunks),
        out_shape=jax.ShapeDtypeStruct((rows, w_all.shape[-1]), jnp.bfloat16),
        in_specs=[vmem] * 3,
        out_specs=vmem,
        scratch_shapes=[
            pltpu.VMEM((heads, subs, rows, width), jnp.bfloat16),
            pltpu.VMEM((rows, w_all.shape[-1]), jnp.float32),
            pltpu.SemaphoreType.DMA((heads, 2, chunks)),
            pltpu.SemaphoreType.DMA((heads, subs, 2, chunks)),
        ],
        compiler_params=pltpu.CompilerParams(
            collective_id=1, has_side_effects=True, vmem_limit_bytes=40 * 1024 * 1024
        ),
        name="mix",
    )(attention, w_all, gate)


def modulate(tokens, modulation):
    values = tokens.astype(jnp.float32)
    center = jnp.mean(values, axis=-1, keepdims=True)
    spread = jnp.mean(jnp.square(values - center), axis=-1, keepdims=True)
    normed = (values - center) * lax.rsqrt(spread + EPSILON)
    return (normed * (1.0 + modulation[1]) + modulation[0]).astype(jnp.bfloat16)


def shards(tokens, modulation, w_qkv, w_out, pattern, counts, spatial_mask):
    row_count, feature_width = tokens.shape
    pairs_local = w_qkv.shape[1]
    head_size = w_qkv.shape[2] // 6
    frames_local = spatial_mask.shape[0]
    positions = row_count // frames_local
    slot_total = pattern.shape[1]
    scale_factor = 1.0 / math.sqrt(head_size)
    hidden = modulate(tokens, modulation)
    projected, whole_out = project(hidden, w_qkv.reshape(w_qkv.shape[0], -1), w_out)
    packed = projected.reshape(
        frames_local, positions, pairs_local, 6 * head_size
    )
    temporal_in = packed[..., : 3 * head_size].transpose(1, 0, 2, 3)
    received = lax.all_to_all(temporal_in, "seq", split_axis=0, concat_axis=1, tiled=True)
    position_span, frame_total, items, _ = received.shape
    relaid = received.reshape(position_span * frame_total, items, 3 * head_size)
    extended = with_halo(relaid[:, :, head_size:], (("seq", 0),), WIN * BLOCK)
    block_count = position_span * frame_total // BLOCK
    key_table = extended.reshape(block_count + 2 * WIN, BLOCK, items, 2 * head_size)
    queries = relaid[:, :, :head_size].reshape(block_count, BLOCK, items, head_size)
    offsets = pattern - (lax.axis_index("seq") * block_count - WIN)

    def slot_step(slot_index, state_pair):
        numerator, denominator = state_pair
        chosen = lax.dynamic_index_in_dim(offsets, slot_index, 1, keepdims=False)
        picked = jnp.take(key_table, chosen, axis=0)
        scores = (
            jnp.einsum(
                "bqnc,bknc->bnqk",
                queries,
                picked[..., :head_size],
                preferred_element_type=jnp.float32,
            )
            * scale_factor
        )
        alive = (slot_index < counts).astype(jnp.float32)
        weights = jnp.exp(scores) * alive[:, None, None, None]
        numerator = numerator + jnp.einsum(
            "bnqk,bknc->bnqc",
            weights.astype(jnp.bfloat16),
            picked[..., head_size:],
            preferred_element_type=jnp.float32,
        )
        return (numerator, denominator + jnp.sum(weights, axis=-1))

    start_state = (
        jnp.zeros((block_count, items, BLOCK, head_size), jnp.float32),
        jnp.zeros((block_count, items, BLOCK), jnp.float32),
    )
    numerator, denominator = lax.fori_loop(0, slot_total, slot_step, start_state)
    outcome = (numerator / denominator[..., None]).astype(jnp.bfloat16)
    outcome = outcome.transpose(0, 2, 1, 3).reshape(position_span, frame_total, items, head_size)
    temporal_out = lax.all_to_all(outcome, "seq", split_axis=1, concat_axis=0, tiled=True)
    spatial = packed[..., 3 * head_size :]
    blocks_frame = positions // BLOCK
    scores = (
        jnp.einsum(
            "fpnc,fqnc->fnpq",
            spatial[..., :head_size],
            spatial[..., head_size : 2 * head_size],
            preferred_element_type=jnp.float32,
        )
        * scale_factor
    )
    keep = spatial_mask.astype(jnp.float32)[:, None, :, None, :, None]
    weights = (
        jnp.exp(scores).reshape(frames_local, pairs_local, blocks_frame, BLOCK, blocks_frame, BLOCK)
        * keep
    )
    weights = weights.reshape(frames_local, pairs_local, positions, positions)
    denominator = jnp.sum(weights, axis=-1)
    numerator = jnp.einsum(
        "fnpq,fqnc->fpnc",
        weights.astype(jnp.bfloat16),
        spatial[..., 2 * head_size :],
        preferred_element_type=jnp.float32,
    )
    spatial_out = (numerator / denominator.transpose(0, 2, 1)[..., None]).astype(jnp.bfloat16)
    attention = jnp.concatenate([temporal_out.transpose(1, 0, 2, 3), spatial_out], axis=-1)
    attention = attention.reshape(row_count, pairs_local * 2 * head_size)
    out_width = w_out.shape[1]
    blocks = lax.axis_size("head") * lax.axis_size("sub")
    gate_slice = lax.dynamic_slice_in_dim(
        modulation[2], lax.axis_index(("head", "sub")) * out_width, out_width, 0
    )
    return mix(attention, whole_out.reshape(blocks, -1, out_width), gate_slice[None, :])

def meet(axes):
    barrier = pltpu.get_barrier_semaphore()
    others = 0
    for axis in axes:
        size = lax.axis_size(axis)
        for hop in range(1, size):
            other = lax.rem(lax.axis_index(axis) + hop, size)
            pl.semaphore_signal(barrier, inc=1, device_id={axis: other}, device_id_type=MESH)
            others += 1
    pl.semaphore_wait(barrier, others)


def push(source, target, send_sem, recv_sem, axis, place):
    return pltpu.make_async_remote_copy(
        src_ref=source,
        dst_ref=target,
        send_sem=send_sem,
        recv_sem=recv_sem,
        device_id={axis: place},
        device_id_type=MESH,
    )


def by_head_kernel(
    sizes, chunks, o_chunks, span, hid_own, w_own, o_own, lists, gate, update,
    hfull, wfull, blocks, o_all, lists_all, table, own, slots, total,
    w_sems, l_sems, z_sems, x_sems, c_sems, o_sems, own_sems, sz_sems, sx_sems, sc_sems,
):
    count, parts, heads, subs = sizes
    me, group = lax.axis_index("seq"), lax.axis_index("groups")
    head, sub = lax.axis_index("head"), lax.axis_index("sub")
    meet(("seq", "groups", "head", "sub"))
    quarter = hid_own.shape[0]
    size = quarter // chunks
    half = w_own.shape[0] // parts
    width = wfull.shape[2]
    mine = pl.ds(pl.multiple_of(group * half, half), half)

    def place(hop, axis, size_):
        return lax.rem(lax.axis_index(axis) + hop, size_)

    def source_of(hop):
        return lax.rem(me + count - hop, count)

    def w_part(other):
        return pl.ds(pl.multiple_of(other * width, width), width)

    def w_along(hop, shard):
        return push(
            w_own.at[mine, w_part(place(hop, "seq", count))], wfull.at[shard, mine],
            w_sems.at[0, 0, hop], w_sems.at[0, 1, hop], "seq", place(hop, "seq", count),
        )

    def w_across(hop, turn):
        spot = wfull.at[source_of(hop), mine]
        return push(
            spot, spot, w_sems.at[turn, 0, hop], w_sems.at[turn, 1, hop],
            "groups", place(turn, "groups", parts),
        )

    def l_along(hop):
        return push(
            lists, lists_all.at[me], l_sems.at[0, hop], l_sems.at[1, hop],
            "seq", place(hop, "seq", count),
        )

    def rows_of(head_hop, sub_hop, chunk):
        owner = lax.rem(head + heads - head_hop, heads) * subs + lax.rem(sub + subs - sub_hop, subs)
        return pl.ds(pl.multiple_of(owner * quarter + chunk * size, size), size)

    def spot(shard, head_hop, sub_hop, chunk):
        return hfull.at[shard, rows_of(head_hop, sub_hop, chunk)]

    def z_push(shard, chunk, way, own):
        target = spot(shard, 0, 0, chunk)
        return push(
            hid_own.at[pl.ds(chunk * size, size)] if own else target, target,
            z_sems.at[way, 0, shard, chunk], z_sems.at[way, 1, shard, chunk],
            "seq", me + (1 if way == 0 else -1),
        )

    def x_push(shard, chunk, hop, own=False):
        target = spot(shard, 0, 0, chunk)
        return push(
            hid_own.at[pl.ds(chunk * size, size)] if own else target, target,
            x_sems.at[hop, 0, shard, chunk], x_sems.at[hop, 1, shard, chunk],
            "head", place(hop, "head", heads),
        )

    def c_push(shard, chunk, hop, turn, own=False):
        target = spot(shard, hop, 0, chunk)
        return push(
            hid_own.at[pl.ds(chunk * size, size)] if own else target, target,
            c_sems.at[hop, turn, 0, shard, chunk], c_sems.at[hop, turn, 1, shard, chunk],
            "sub", place(turn, "sub", subs),
        )

    outs = LineGather(o_own, o_all, o_sems, o_chunks, count, parts)
    onward, shard_of, present = outs.onward, outs.shard_of, outs.present
    ways = lambda step: (0, 1) if step else (0,)

    for hop in range(1, count):
        l_along(hop).start()
    for hop in range(1, count):
        w_along(hop, me).start()
    for chunk in range(chunks):
        for way in (0, 1):
            @pl.when(onward(way))
            def _():
                z_push(me, chunk, way, True).start()
        for hop in range(1, heads):
            x_push(me, chunk, hop, True).start()
        for turn in range(1, subs):
            c_push(me, chunk, 0, turn, True).start()
    keeps = [
        pltpu.make_async_copy(o_own, o_all.at[me], own_sems.at[0]),
        pltpu.make_async_copy(w_own.at[:, w_part(me)], wfull.at[me], own_sems.at[1]),
        pltpu.make_async_copy(
            hid_own,
            hfull.at[me, pl.ds(pl.multiple_of((head * subs + sub) * quarter, quarter), quarter)],
            own_sems.at[2],
        ),
        pltpu.make_async_copy(lists, lists_all.at[me], own_sems.at[3]),
    ]
    for keep in keeps:
        keep.start()

    for hop in range(1, count):
        w_along(hop, source_of(hop)).wait_recv()
        for turn in range(1, parts):
            w_across(hop, turn).start()

    def z_relay(step):
        for chunk in range(chunks):
            for way in ways(step):
                shard = shard_of(step, way)

                @pl.when(present(step, way))
                def _():
                    z_push(shard, chunk, way, False).wait_recv()

                    @pl.when(onward(way))
                    def _():
                        z_push(shard, chunk, way, False).start()

                    for hop in range(1, heads):
                        x_push(shard, chunk, hop).start()
                    for turn in range(1, subs):
                        c_push(shard, chunk, 0, turn).start()

    def x_relay(step):
        for chunk in range(chunks):
            for way in ways(step):
                shard = shard_of(step, way)

                @pl.when(present(step, way))
                def _():
                    for hop in range(1, heads):
                        x_push(shard, chunk, hop).wait_recv()
                        for turn in range(1, subs):
                            c_push(shard, chunk, hop, turn).start()

    def finish(step):
        for way in ways(step):
            shard = shard_of(step, way)

            @pl.when(present(step, way))
            def _():
                for chunk in range(chunks):
                    for hop in range(heads):
                        for turn in range(1, subs):
                            c_push(shard, chunk, hop, turn).wait_recv()
                weight = wfull[...].reshape(-1, wfull.shape[-1])
                total = jnp.dot(hfull[shard], weight, preferred_element_type=jnp.float32)
                total = total.astype(blocks.dtype)
                rows = total.shape[0]

                @pl.when(lax.rem(me, 2) == 0)
                def _():
                    at = pl.ds(pl.multiple_of(shard * span, span), span)
                    for i in range(rows // span):
                        blocks[i, at, :] = total[i * span : (i + 1) * span]

                @pl.when(lax.rem(me, 2) == 1)
                def _():
                    each = blocks.shape[1]
                    for i in range(rows // each):
                        blocks[shard * (rows // each) + i] = total[i * each : (i + 1) * each]

    for step in range(1, count):
        z_relay(step)
        if step == count - 1:
            outs.open_line()
        if step == 2:
            for keep in keeps:
                keep.wait()
            for hop in range(1, count):
                for turn in range(1, parts):
                    w_across(hop, turn).wait_recv()
        if step >= 2:
            x_relay(step - 2)
            finish(step - 2)
    x_relay(count - 2)
    outs.relay(1)
    finish(count - 2)
    x_relay(count - 1)
    finish(count - 1)
    for hop in range(1, count):
        l_along(hop).wait_recv()
    to_table = pltpu.make_async_copy(lists_all, table, own_sems.at[4])
    to_table.start()
    to_table.wait()
    scale = 1.0 / math.sqrt(own.shape[2])
    attend(count, span, scale, lax.rem(me, 2), table, blocks, own)
    spread(
        count, heads, subs, outs, own, o_all, gate, update, slots, total,
        sz_sems, sx_sems, sc_sems, own_sems.at[5],
    )

    for hop in range(1, count):
        l_along(hop).wait_send()
        w_along(hop, me).wait_send()
        for turn in range(1, parts):
            w_across(hop, turn).wait_send()
    for step in range(count):
        for way in ways(step):
            shard = shard_of(step, way)

            @pl.when(present(step, way))
            def _():
                for chunk in range(chunks):
                    for side in (0, 1) if step == 0 else (way,):
                        @pl.when(onward(side))
                        def _():
                            z_push(shard, chunk, side, False).wait_send()
                    for hop in range(1, heads):
                        x_push(shard, chunk, hop).wait_send()
                    for hop in range(heads):
                        for turn in range(1, subs):
                            c_push(shard, chunk, hop, turn).wait_send()
    for step in range(1, count):
        outs.close_sends(step)
    outs.close_own()


def by_head(hid_own, w_own, o_own, lists, gate, span, block):
    sizes = tuple(lax.axis_size(axis) for axis in ("seq", "groups", "head", "sub"))
    count, parts, heads, subs = sizes
    rows = hid_own.shape[0] * heads * subs
    depth, width = hid_own.shape[1], w_own.shape[1] // count
    chunks = pieces_of(hid_own.shape[0], 2)
    o_chunks = pieces_of(o_own.shape[0] // parts, 2)
    vmem = pl.BlockSpec(memory_space=pltpu.VMEM)
    dma = pltpu.SemaphoreType.DMA
    return pl.pallas_call(
        functools.partial(by_head_kernel, sizes, chunks, o_chunks, span),
        out_shape=jax.ShapeDtypeStruct((rows, o_own.shape[1]), jnp.bfloat16),
        in_specs=[vmem] * 5,
        out_specs=vmem,
        scratch_shapes=[
            pltpu.VMEM((count, rows, depth), jnp.bfloat16),
            pltpu.VMEM((count, w_own.shape[0], width), jnp.bfloat16),
            pltpu.VMEM((count * rows // block, block, width), jnp.bfloat16),
            pltpu.VMEM((count,) + o_own.shape, jnp.bfloat16),
            pltpu.VMEM((count,) + lists.shape, lists.dtype),
            pltpu.SMEM((count,) + lists.shape, lists.dtype),
            pltpu.VMEM((count, rows, width // 3), jnp.bfloat16),
            pltpu.VMEM((heads, subs, rows, count * width // 3), jnp.bfloat16),
            pltpu.VMEM((rows, o_own.shape[1]), jnp.float32),
            dma((parts, 2, count)),
            dma((2, count)),
            dma((2, 2, count, chunks)),
            dma((heads, 2, count, chunks)),
            dma((heads, subs, 2, count, chunks)),
            dma((1 + parts, 2, count, o_chunks)),
            dma((6,)),
            dma((2, count)),
            dma((heads, 2, count)),
            dma((heads, subs, 2, count)),
        ],
        compiler_params=pltpu.CompilerParams(
            collective_id=2, has_side_effects=True, vmem_limit_bytes=56 * 1024 * 1024
        ),
        name="by_head",
    )(hid_own, w_own, o_own, lists, gate)


def attend(count, span, scale, role, table, blocks, out):
    total, block, width = blocks.shape
    size = width // 3
    each = total // count
    slots = each

    def query(b, carry):
        device, row = b // each, lax.rem(b, each)
        used = table[device, 0, each * slots + row]
        q = blocks[b, :, :size]
        numerator = jnp.zeros((block, size), jnp.float32)
        denominator = jnp.zeros((block, 1), jnp.float32)
        for j in range(slots):
            listed = table[device, 0, row * slots + j]
            seen = table[device, 0, each * (slots + 1) + row * slots + j]
            at = jnp.where(role == 0, listed, device * each + j)
            alive = jnp.where(role == 0, jnp.where(j < used, 1.0, 0.0), jnp.where(seen > 0, 1.0, 0.0))
            scores = lax.dot_general(
                q, blocks[at, :, size : 2 * size], (((1,), (1,)), ((), ())),
                preferred_element_type=jnp.float32,
            )
            weights = jnp.exp(scores * scale) * alive
            denominator = denominator + jnp.sum(weights, axis=-1, keepdims=True)
            numerator = numerator + jnp.dot(
                weights.astype(jnp.bfloat16), blocks[at, :, 2 * size :],
                preferred_element_type=jnp.float32,
            )
        result = (numerator / denominator).astype(out.dtype)

        @pl.when(role == 0)
        def _():
            at = pl.ds(pl.multiple_of(b * span, span), span)
            for f in range(count):
                out[f, at, :] = result[f * span : (f + 1) * span]

        @pl.when(role == 1)
        def _():
            out[device, pl.ds(pl.multiple_of(row * block, block), block), :] = result

        return carry

    lax.fori_loop(0, total, query, 0, unroll=2)


def spread(
    count, heads, subs, outs, own, w_all, gate, update, slots, total, z_sems, x_sems, c_sems, own_sem
):
    me, head, sub = (lax.axis_index(axis) for axis in ("seq", "head", "sub"))
    size = own.shape[2]

    def columns(step):
        source = lax.rem(me + count - step, count)
        return pl.ds(pl.multiple_of(source * size, size), size)

    def spot(hop, turn, step):
        return slots.at[hop, turn, :, columns(step)]

    def to_seq(step):
        other = lax.rem(me + step, count)
        return push(
            own.at[other], spot(0, 0, 0), z_sems.at[0, step], z_sems.at[1, step], "seq", other
        )

    def to_head(hop, step):
        return push(
            own.at[me] if step == 0 else spot(0, 0, step), spot(hop, 0, step),
            x_sems.at[hop, 0, step], x_sems.at[hop, 1, step],
            "head", lax.rem(head + hop, heads),
        )

    def to_sub(hop, turn, step):
        return push(
            own.at[me] if hop == 0 and step == 0 else spot(hop, 0, step), spot(hop, turn, step),
            c_sems.at[hop, turn, 0, step], c_sems.at[hop, turn, 1, step],
            "sub", lax.rem(sub + turn, subs),
        )

    def hand_over(step):
        for hop in range(1, heads):
            to_head(hop, step).start()
        for turn in range(1, subs):
            to_sub(0, turn, step).start()

    def pass_on(step):
        for hop in range(1, heads):
            to_head(hop, step).wait_recv()
            for turn in range(1, subs):
                to_sub(hop, turn, step).start()

    for step in range(1, count):
        to_seq(step).start()
    hand_over(0)
    keep = pltpu.make_async_copy(own.at[me], spot(0, 0, 0), own_sem)
    keep.start()
    for step in range(1, count):
        if step > 1:
            outs.relay(step)
        to_seq(step).wait_recv()
        hand_over(step)
        pass_on(step - 1)
    keep.wait()

    def add(hop, turn, first):
        owner = lax.rem(head + heads - hop, heads) * subs + lax.rem(sub + subs - turn, subs)
        product = jnp.dot(slots[hop, turn], w_all[owner], preferred_element_type=jnp.float32)
        total[...] = product if first else total[...] + product

    pass_on(count - 1)
    for step in range(1, count):
        for way in (0, 1):
            @pl.when(outs.present(step, way))
            def _():
                outs.complete(outs.shard_of(step, way))
    add(0, 0, True)
    for hop in range(heads):
        if hop:
            add(hop, 0, False)
        for turn in range(1, subs):
            for step in range(count):
                to_sub(hop, turn, step).wait_recv()
            add(hop, turn, False)
    update[...] = (gate[...] * total[...]).astype(update.dtype)
    for step in range(count):
        if step:
            to_seq(step).wait_send()
        for hop in range(1, heads):
            to_head(hop, step).wait_send()
        for hop in range(heads):
            for turn in range(1, subs):
                to_sub(hop, turn, step).wait_send()


def shards_by_head(tokens, modulation, w_qkv, w_out, pattern, counts, spatial_mask):
    count = lax.axis_size("seq")
    blocks = lax.axis_size("head") * lax.axis_size("sub")
    row_count = tokens.shape[0]
    depth = w_qkv.shape[0]
    quarter = row_count // blocks
    place = lax.axis_index(("head", "sub"))
    span = BLOCK // count
    hid_own = modulate(lax.dynamic_slice_in_dim(tokens, place * quarter, quarter, 0), modulation)
    entries = jnp.concatenate([pattern.reshape(-1), counts.reshape(-1), spatial_mask.reshape(-1)])
    lists = jnp.pad(entries, (0, 8 * 128 - entries.shape[0])).reshape(8, 128)
    out_width = w_out.shape[1]
    gate_slice = lax.dynamic_slice_in_dim(modulation[2], place * out_width, out_width, 0)
    return by_head(
        hid_own, w_qkv.reshape(depth, -1), w_out, lists, gate_slice[None, :], span, BLOCK
    )


def one_head_each(mesh_count, blocks, tokens, w_qkv, pattern, spatial_mask):
    rows, frames = tokens.shape[0], spatial_mask.shape[0]
    return (
        w_qkv.shape[1] * 2 == mesh_count > 2
        and frames == 1
        and mesh_count == blocks
        and pattern.shape[0] == pattern.shape[1] == spatial_mask.shape[1]
        and 2 * pattern.size + pattern.shape[0] <= 128
        and spatial_mask.shape[2] == pattern.shape[1]
        and rows == BLOCK * spatial_mask.shape[1]
        and BLOCK % (16 * mesh_count) == 0
        and w_qkv.shape[0] % 128 == 0
        and rows % (16 * blocks) == 0
    )


def shards_any(*args):
    tokens, _, w_qkv, _, pattern, _, spatial_mask = args
    blocks = lax.axis_size("head") * lax.axis_size("sub")
    if one_head_each(lax.axis_size("seq"), blocks, tokens, w_qkv, pattern, spatial_mask):
        return shards_by_head(*args)
    return shards(*args)


def solution(mesh):
    return jax.shard_map(
        shards_any,
        mesh=mesh,
        in_specs=(
            P(("groups", "seq"), None),
            P(),
            P("seq", ("head", "sub"), None),
            P("seq", ("head", "sub")),
            P(("groups", "seq"), None),
            P(("groups", "seq")),
            P(("groups", "seq"), None, None),
        ),
        out_specs=P(("groups", "seq"), ("head", "sub")),
        check_vma=False,
    )
```

```python
import functools
import math

import jax
import jax.numpy as jnp
from jax import lax
from jax.experimental import pallas as pl
from jax.experimental.pallas import tpu as pltpu
from jax.sharding import PartitionSpec as P

BLOCK = 128
WIN = 2


EPSILON = 1e-06


def with_halo(cells, sides, width):
    for axis, dim in sides:
        count = lax.axis_size(axis)
        ends = count - 1
        head = lax.slice_in_dim(cells, 0, width, axis=dim)
        tail = lax.slice_in_dim(cells, cells.shape[dim] - width, cells.shape[dim], axis=dim)
        cells = jnp.concatenate(
            [
                lax.ppermute(tail, axis, [(i, (i + 1) % count) for i in range(ends)]),
                cells,
                lax.ppermute(head, axis, [((i + 1) % count, i) for i in range(ends)]),
            ],
            axis=dim,
        )
    return cells


MESH = pl.DeviceIdType.MESH


def pieces_of(rows, most=4):
    for count in range(most, 0, -1):
        if rows % (16 * count) == 0:
            return count
    return 1


class LineGather:
    def __init__(self, own, slots, sems, chunks, count, parts):
        self.own, self.slots, self.chunks = own, slots, chunks
        self.sems, self.count, self.parts = sems, count, parts
        self.me = lax.axis_index("seq")
        self.group = lax.axis_index("groups")
        self.size = own.shape[0] // (parts * chunks)

    def rows(self, group, chunk):
        start = (group * self.chunks + chunk) * self.size
        return pl.ds(pl.multiple_of(start, self.size), self.size)

    def along(self, shard, chunk, way, own):
        rows = self.rows(self.group, chunk)
        source = self.own.at[rows] if own else self.slots.at[shard, rows]
        return pltpu.make_async_remote_copy(
            src_ref=source,
            dst_ref=self.slots.at[shard, rows],
            send_sem=self.sems.at[way, 0, shard, chunk],
            recv_sem=self.sems.at[way, 1, shard, chunk],
            device_id={"seq": self.me + (1 if way == 0 else -1)},
            device_id_type=MESH,
        )

    def across(self, shard, chunk, hop):
        rows = self.rows(self.group, chunk)
        return pltpu.make_async_remote_copy(
            src_ref=self.slots.at[shard, rows],
            dst_ref=self.slots.at[shard, rows],
            send_sem=self.sems.at[1 + hop, 0, shard, chunk],
            recv_sem=self.sems.at[1 + hop, 1, shard, chunk],
            device_id={"groups": lax.rem(self.group + hop, self.parts)},
            device_id_type=MESH,
        )

    def open_line(self):
        for chunk in range(self.chunks):
            for way in (0, 1):
                @pl.when(self.onward(way))
                def _():
                    self.along(self.me, chunk, way, True).start()

    def onward(self, way):
        return self.me < self.count - 1 if way == 0 else self.me > 0

    def shard_of(self, step, way):
        return self.me - step if way == 0 else self.me + step

    def present(self, step, way):
        return self.me >= step if way == 0 else self.me + step < self.count

    def relay(self, step):
        for chunk in range(self.chunks):
            for way in (0, 1):
                shard = self.shard_of(step, way)

                @pl.when(self.present(step, way))
                def _():
                    self.along(shard, chunk, way, False).wait_recv()

                    @pl.when(self.onward(way))
                    def _():
                        self.along(shard, chunk, way, False).start()

                    for hop in range(1, self.parts):
                        self.across(shard, chunk, hop).start()

    def complete(self, shard):
        for chunk in range(self.chunks):
            for hop in range(1, self.parts):
                self.across(shard, chunk, hop).wait_recv()

    def close_sends(self, step):
        for chunk in range(self.chunks):
            for way in (0, 1):
                shard = self.shard_of(step, way)

                @pl.when(self.present(step, way))
                def _():
                    @pl.when(self.onward(way))
                    def _():
                        self.along(shard, chunk, way, False).wait_send()

                    for hop in range(1, self.parts):
                        self.across(shard, chunk, hop).wait_send()

    def close_own(self):
        for chunk in range(self.chunks):
            for way in (0, 1):
                @pl.when(self.onward(way))
                def _():
                    self.along(self.me, chunk, way, True).wait_send()


def project_kernel(count, parts, q_chunks, o_chunks, hidden, w_own, o_own, qkv, o_all, slots, total, q_sems, o_sems, own_sem):
    me = lax.axis_index("seq")
    group = lax.axis_index("groups")
    barrier = pltpu.get_barrier_semaphore()

    @pl.when(me > 0)
    def _():
        pl.semaphore_signal(barrier, inc=1, device_id={"seq": me - 1}, device_id_type=MESH)

    @pl.when(me < count - 1)
    def _():
        pl.semaphore_signal(barrier, inc=1, device_id={"seq": me + 1}, device_id_type=MESH)

    for hop in range(1, parts):
        pl.semaphore_signal(
            barrier, inc=1, device_id={"groups": lax.rem(group + hop, parts)}, device_id_type=MESH
        )
    neighbours = jnp.where(me > 0, 1, 0) + jnp.where(me < count - 1, 1, 0) + (parts - 1)
    pl.semaphore_wait(barrier, neighbours)

    line = LineGather(w_own, slots, q_sems, q_chunks, count, parts)
    outs = LineGather(o_own, o_all, o_sems, o_chunks, count, parts)
    line.open_line()
    keep = pltpu.make_async_copy(o_own, o_all.at[me], own_sem)
    keep.start()
    tile = 256

    def add(shard, block, first):
        def column(j, carry):
            at = pl.ds(pl.multiple_of(j * tile, tile), tile)
            product = jnp.dot(hidden[shard], block[:, at], preferred_element_type=jnp.float32)
            total[:, at] = product if first else total[:, at] + product
            return carry

        lax.fori_loop(0, total.shape[1] // tile, column, 0)

    def finish(step):
        for way in (0, 1):
            shard = line.shard_of(step, way)

            @pl.when(line.present(step, way))
            def _():
                line.complete(shard)
                add(shard, slots.at[shard], False)

    add(me, w_own, True)

    def q_step(step, carry):
        line.relay(step)

        @pl.when(step > 1)
        def _():
            finish(step - 1)

        return carry

    lax.fori_loop(1, count, q_step, 0)
    outs.open_line()
    finish(count - 1)
    qkv[...] = total[...].astype(qkv.dtype)

    def o_step(step, carry):
        outs.relay(step)
        return carry

    lax.fori_loop(1, count, o_step, 0)

    def last(step, carry):
        line.close_sends(step)
        outs.close_sends(step)
        for way in (0, 1):
            shard = outs.shard_of(step, way)

            @pl.when(outs.present(step, way))
            def _():
                outs.complete(shard)

        return carry

    lax.fori_loop(1, count, last, 0)
    line.close_own()
    outs.close_own()
    keep.wait()


def project(hidden, w_own, o_own):
    count, parts = lax.axis_size("seq"), lax.axis_size("groups")
    rows, depth = hidden.shape
    hidden = hidden.reshape(rows, count, depth // count).transpose(1, 0, 2)
    width = w_own.shape[1]
    most = 4 if count <= 8 else 1
    q_chunks = pieces_of(w_own.shape[0] // parts, most)
    o_chunks = pieces_of(o_own.shape[0] // parts, most)
    vmem = pl.BlockSpec(memory_space=pltpu.VMEM)
    return pl.pallas_call(
        functools.partial(project_kernel, count, parts, q_chunks, o_chunks),
        out_shape=[
            jax.ShapeDtypeStruct((rows, width), jnp.bfloat16),
            jax.ShapeDtypeStruct((count,) + o_own.shape, jnp.bfloat16),
        ],
        in_specs=[vmem] * 3,
        out_specs=[vmem, pl.BlockSpec(memory_space=pl.ANY)],
        scratch_shapes=[
            pltpu.VMEM((count,) + w_own.shape, jnp.bfloat16),
            pltpu.VMEM((rows, width), jnp.float32),
            pltpu.SemaphoreType.DMA((1 + parts, 2, count, q_chunks)),
            pltpu.SemaphoreType.DMA((1 + parts, 2, count, o_chunks)),
            pltpu.SemaphoreType.DMA,
        ],
        compiler_params=pltpu.CompilerParams(
            collective_id=0, has_side_effects=True, vmem_limit_bytes=48 * 1024 * 1024
        ),
        name="project",
    )(hidden, w_own, o_own)


def mix_kernel(heads, subs, chunks, attn, w_all, gate, update, slots, total, x_sems, c_sems):
    head, sub = lax.axis_index("head"), lax.axis_index("sub")
    barrier = pltpu.get_barrier_semaphore()
    for hop in range(1, heads):
        pl.semaphore_signal(
            barrier, inc=1, device_id={"head": lax.rem(head + hop, heads)}, device_id_type=MESH
        )
    for hop in range(1, subs):
        pl.semaphore_signal(
            barrier, inc=1, device_id={"sub": lax.rem(sub + hop, subs)}, device_id_type=MESH
        )
    pl.semaphore_wait(barrier, heads + subs - 2)
    size = attn.shape[0] // chunks

    def to_head(hop, chunk):
        rows = pl.ds(chunk * size, size)
        return pltpu.make_async_remote_copy(
            src_ref=attn.at[rows],
            dst_ref=slots.at[hop, 0, rows],
            send_sem=x_sems.at[hop, 0, chunk],
            recv_sem=x_sems.at[hop, 1, chunk],
            device_id={"head": lax.rem(head + hop, heads)},
            device_id_type=MESH,
        )

    def to_sub(hop, turn, chunk):
        rows = pl.ds(chunk * size, size)
        return pltpu.make_async_remote_copy(
            src_ref=attn.at[rows] if hop == 0 else slots.at[hop, 0, rows],
            dst_ref=slots.at[hop, turn, rows],
            send_sem=c_sems.at[hop, turn, 0, chunk],
            recv_sem=c_sems.at[hop, turn, 1, chunk],
            device_id={"sub": lax.rem(sub + turn, subs)},
            device_id_type=MESH,
        )

    for chunk in range(chunks):
        for hop in range(1, heads):
            to_head(hop, chunk).start()
        for turn in range(1, subs):
            to_sub(0, turn, chunk).start()

    def add(chunk, hop, turn, first):
        rows = slice(chunk * size, (chunk + 1) * size)
        owner = lax.rem(head + heads - hop, heads) * subs + lax.rem(sub + subs - turn, subs)
        block = attn[rows, :] if hop == 0 and turn == 0 else slots[hop, turn, rows, :]
        product = jnp.dot(block, w_all[owner], preferred_element_type=jnp.float32)
        total[rows, :] = product if first else total[rows, :] + product

    for chunk in range(chunks):
        add(chunk, 0, 0, True)
    for chunk in range(chunks):
        for turn in range(1, subs):
            to_sub(0, turn, chunk).wait_recv()
            add(chunk, 0, turn, False)
    for chunk in range(chunks):
        for hop in range(1, heads):
            to_head(hop, chunk).wait_recv()
            for turn in range(1, subs):
                to_sub(hop, turn, chunk).start()
            add(chunk, hop, 0, False)
    for chunk in range(chunks):
        for hop in range(1, heads):
            for turn in range(1, subs):
                to_sub(hop, turn, chunk).wait_recv()
                add(chunk, hop, turn, False)
        rows = slice(chunk * size, (chunk + 1) * size)
        update[rows, :] = (gate[...] * total[rows, :]).astype(update.dtype)
    for chunk in range(chunks):
        for hop in range(1, heads):
            to_head(hop, chunk).wait_send()
        for hop in range(heads):
            for turn in range(1, subs):
                to_sub(hop, turn, chunk).wait_send()


def mix(attention, w_all, gate):
    heads, subs = lax.axis_size("head"), lax.axis_size("sub")
    rows, width = attention.shape
    chunks = pieces_of(rows, 2)
    vmem = pl.BlockSpec(memory_space=pltpu.VMEM)
    return pl.pallas_call(
        functools.partial(mix_kernel, heads, subs, chunks),
        out_shape=jax.ShapeDtypeStruct((rows, w_all.shape[-1]), jnp.bfloat16),
        in_specs=[vmem] * 3,
        out_specs=vmem,
        scratch_shapes=[
            pltpu.VMEM((heads, subs, rows, width), jnp.bfloat16),
            pltpu.VMEM((rows, w_all.shape[-1]), jnp.float32),
            pltpu.SemaphoreType.DMA((heads, 2, chunks)),
            pltpu.SemaphoreType.DMA((heads, subs, 2, chunks)),
        ],
        compiler_params=pltpu.CompilerParams(
            collective_id=1, has_side_effects=True, vmem_limit_bytes=40 * 1024 * 1024
        ),
        name="mix",
    )(attention, w_all, gate)


def modulate(tokens, modulation):
    values = tokens.astype(jnp.float32)
    center = jnp.mean(values, axis=-1, keepdims=True)
    spread = jnp.mean(jnp.square(values - center), axis=-1, keepdims=True)
    normed = (values - center) * lax.rsqrt(spread + EPSILON)
    return (normed * (1.0 + modulation[1]) + modulation[0]).astype(jnp.bfloat16)


def shards(tokens, modulation, w_qkv, w_out, pattern, counts, spatial_mask):
    row_count, feature_width = tokens.shape
    pairs_local = w_qkv.shape[1]
    head_size = w_qkv.shape[2] // 6
    frames_local = spatial_mask.shape[0]
    positions = row_count // frames_local
    slot_total = pattern.shape[1]
    scale_factor = 1.0 / math.sqrt(head_size)
    hidden = modulate(tokens, modulation)
    projected, whole_out = project(hidden, w_qkv.reshape(w_qkv.shape[0], -1), w_out)
    packed = projected.reshape(
        frames_local, positions, pairs_local, 6 * head_size
    )
    temporal_in = packed[..., : 3 * head_size].transpose(1, 0, 2, 3)
    received = lax.all_to_all(temporal_in, "seq", split_axis=0, concat_axis=1, tiled=True)
    position_span, frame_total, items, _ = received.shape
    relaid = received.reshape(position_span * frame_total, items, 3 * head_size)
    extended = with_halo(relaid[:, :, head_size:], (("seq", 0),), WIN * BLOCK)
    block_count = position_span * frame_total // BLOCK
    key_table = extended.reshape(block_count + 2 * WIN, BLOCK, items, 2 * head_size)
    queries = relaid[:, :, :head_size].reshape(block_count, BLOCK, items, head_size)
    offsets = pattern - (lax.axis_index("seq") * block_count - WIN)

    def slot_step(slot_index, state_pair):
        numerator, denominator = state_pair
        chosen = lax.dynamic_index_in_dim(offsets, slot_index, 1, keepdims=False)
        picked = jnp.take(key_table, chosen, axis=0)
        scores = (
            jnp.einsum(
                "bqnc,bknc->bnqk",
                queries,
                picked[..., :head_size],
                preferred_element_type=jnp.float32,
            )
            * scale_factor
        )
        alive = (slot_index < counts).astype(jnp.float32)
        weights = jnp.exp(scores) * alive[:, None, None, None]
        numerator = numerator + jnp.einsum(
            "bnqk,bknc->bnqc",
            weights.astype(jnp.bfloat16),
            picked[..., head_size:],
            preferred_element_type=jnp.float32,
        )
        return (numerator, denominator + jnp.sum(weights, axis=-1))

    start_state = (
        jnp.zeros((block_count, items, BLOCK, head_size), jnp.float32),
        jnp.zeros((block_count, items, BLOCK), jnp.float32),
    )
    numerator, denominator = lax.fori_loop(0, slot_total, slot_step, start_state)
    outcome = (numerator / denominator[..., None]).astype(jnp.bfloat16)
    outcome = outcome.transpose(0, 2, 1, 3).reshape(position_span, frame_total, items, head_size)
    temporal_out = lax.all_to_all(outcome, "seq", split_axis=1, concat_axis=0, tiled=True)
    spatial = packed[..., 3 * head_size :]
    blocks_frame = positions // BLOCK
    scores = (
        jnp.einsum(
            "fpnc,fqnc->fnpq",
            spatial[..., :head_size],
            spatial[..., head_size : 2 * head_size],
            preferred_element_type=jnp.float32,
        )
        * scale_factor
    )
    keep = spatial_mask.astype(jnp.float32)[:, None, :, None, :, None]
    weights = (
        jnp.exp(scores).reshape(frames_local, pairs_local, blocks_frame, BLOCK, blocks_frame, BLOCK)
        * keep
    )
    weights = weights.reshape(frames_local, pairs_local, positions, positions)
    denominator = jnp.sum(weights, axis=-1)
    numerator = jnp.einsum(
        "fnpq,fqnc->fpnc",
        weights.astype(jnp.bfloat16),
        spatial[..., 2 * head_size :],
        preferred_element_type=jnp.float32,
    )
    spatial_out = (numerator / denominator.transpose(0, 2, 1)[..., None]).astype(jnp.bfloat16)
    attention = jnp.concatenate([temporal_out.transpose(1, 0, 2, 3), spatial_out], axis=-1)
    attention = attention.reshape(row_count, pairs_local * 2 * head_size)
    out_width = w_out.shape[1]
    blocks = lax.axis_size("head") * lax.axis_size("sub")
    gate_slice = lax.dynamic_slice_in_dim(
        modulation[2], lax.axis_index(("head", "sub")) * out_width, out_width, 0
    )
    return mix(attention, whole_out.reshape(blocks, -1, out_width), gate_slice[None, :])

def meet(axes):
    barrier = pltpu.get_barrier_semaphore()
    others = 0
    for axis in axes:
        size = lax.axis_size(axis)
        for hop in range(1, size):
            other = lax.rem(lax.axis_index(axis) + hop, size)
            pl.semaphore_signal(barrier, inc=1, device_id={axis: other}, device_id_type=MESH)
            others += 1
    pl.semaphore_wait(barrier, others)


def push(source, target, send_sem, recv_sem, axis, place):
    return pltpu.make_async_remote_copy(
        src_ref=source,
        dst_ref=target,
        send_sem=send_sem,
        recv_sem=recv_sem,
        device_id={axis: place},
        device_id_type=MESH,
    )


def by_head_kernel(
    sizes, chunks, o_chunks, span, hid_own, w_own, o_own, lists, gate, update,
    hfull, wfull, blocks, o_all, lists_all, table, own, slots, total,
    w_sems, l_sems, z_sems, x_sems, c_sems, o_sems, own_sems, sz_sems, sx_sems, sc_sems,
):
    count, parts, heads, subs = sizes
    me, group = lax.axis_index("seq"), lax.axis_index("groups")
    head, sub = lax.axis_index("head"), lax.axis_index("sub")
    meet(("seq", "groups", "head", "sub"))
    quarter = hid_own.shape[0]
    size = quarter // chunks
    half = w_own.shape[0] // parts
    width = wfull.shape[2]
    mine = pl.ds(pl.multiple_of(group * half, half), half)

    def place(hop, axis, size_):
        return lax.rem(lax.axis_index(axis) + hop, size_)

    def source_of(hop):
        return lax.rem(me + count - hop, count)

    def w_part(other):
        return pl.ds(pl.multiple_of(other * width, width), width)

    def w_along(hop, shard):
        return push(
            w_own.at[mine, w_part(place(hop, "seq", count))], wfull.at[shard, mine],
            w_sems.at[0, 0, hop], w_sems.at[0, 1, hop], "seq", place(hop, "seq", count),
        )

    def w_across(hop, turn):
        spot = wfull.at[source_of(hop), mine]
        return push(
            spot, spot, w_sems.at[turn, 0, hop], w_sems.at[turn, 1, hop],
            "groups", place(turn, "groups", parts),
        )

    def l_along(hop):
        return push(
            lists, lists_all.at[me], l_sems.at[0, hop], l_sems.at[1, hop],
            "seq", place(hop, "seq", count),
        )

    def rows_of(head_hop, sub_hop, chunk):
        owner = lax.rem(head + heads - head_hop, heads) * subs + lax.rem(sub + subs - sub_hop, subs)
        return pl.ds(pl.multiple_of(owner * quarter + chunk * size, size), size)

    def spot(shard, head_hop, sub_hop, chunk):
        return hfull.at[shard, rows_of(head_hop, sub_hop, chunk)]

    def z_push(shard, chunk, way, own):
        target = spot(shard, 0, 0, chunk)
        return push(
            hid_own.at[pl.ds(chunk * size, size)] if own else target, target,
            z_sems.at[way, 0, shard, chunk], z_sems.at[way, 1, shard, chunk],
            "seq", me + (1 if way == 0 else -1),
        )

    def x_push(shard, chunk, hop, own=False):
        target = spot(shard, 0, 0, chunk)
        return push(
            hid_own.at[pl.ds(chunk * size, size)] if own else target, target,
            x_sems.at[hop, 0, shard, chunk], x_sems.at[hop, 1, shard, chunk],
            "head", place(hop, "head", heads),
        )

    def c_push(shard, chunk, hop, turn, own=False):
        target = spot(shard, hop, 0, chunk)
        return push(
            hid_own.at[pl.ds(chunk * size, size)] if own else target, target,
            c_sems.at[hop, turn, 0, shard, chunk], c_sems.at[hop, turn, 1, shard, chunk],
            "sub", place(turn, "sub", subs),
        )

    outs = LineGather(o_own, o_all, o_sems, o_chunks, count, parts)
    onward, shard_of, present = outs.onward, outs.shard_of, outs.present
    ways = lambda step: (0, 1) if step else (0,)

    for hop in range(1, count):
        l_along(hop).start()
    for hop in range(1, count):
        w_along(hop, me).start()
    for chunk in range(chunks):
        for way in (0, 1):
            @pl.when(onward(way))
            def _():
                z_push(me, chunk, way, True).start()
        for hop in range(1, heads):
            x_push(me, chunk, hop, True).start()
        for turn in range(1, subs):
            c_push(me, chunk, 0, turn, True).start()
    keeps = [
        pltpu.make_async_copy(o_own, o_all.at[me], own_sems.at[0]),
        pltpu.make_async_copy(w_own.at[:, w_part(me)], wfull.at[me], own_sems.at[1]),
        pltpu.make_async_copy(
            hid_own,
            hfull.at[me, pl.ds(pl.multiple_of((head * subs + sub) * quarter, quarter), quarter)],
            own_sems.at[2],
        ),
        pltpu.make_async_copy(lists, lists_all.at[me], own_sems.at[3]),
    ]
    for keep in keeps:
        keep.start()

    for hop in range(1, count):
        w_along(hop, source_of(hop)).wait_recv()
        for turn in range(1, parts):
            w_across(hop, turn).start()

    def z_relay(step):
        for chunk in range(chunks):
            for way in ways(step):
                shard = shard_of(step, way)

                @pl.when(present(step, way))
                def _():
                    z_push(shard, chunk, way, False).wait_recv()

                    @pl.when(onward(way))
                    def _():
                        z_push(shard, chunk, way, False).start()

                    for hop in range(1, heads):
                        x_push(shard, chunk, hop).start()
                    for turn in range(1, subs):
                        c_push(shard, chunk, 0, turn).start()

    def x_relay(step):
        for chunk in range(chunks):
            for way in ways(step):
                shard = shard_of(step, way)

                @pl.when(present(step, way))
                def _():
                    for hop in range(1, heads):
                        x_push(shard, chunk, hop).wait_recv()
                        for turn in range(1, subs):
                            c_push(shard, chunk, hop, turn).start()

    def finish(step):
        for way in ways(step):
            shard = shard_of(step, way)

            @pl.when(present(step, way))
            def _():
                for chunk in range(chunks):
                    for hop in range(heads):
                        for turn in range(1, subs):
                            c_push(shard, chunk, hop, turn).wait_recv()
                weight = wfull[...].reshape(-1, wfull.shape[-1])
                total = jnp.dot(hfull[shard], weight, preferred_element_type=jnp.float32)
                total = total.astype(blocks.dtype)
                rows = total.shape[0]

                @pl.when(lax.rem(me, 2) == 0)
                def _():
                    at = pl.ds(pl.multiple_of(shard * span, span), span)
                    for i in range(rows // span):
                        blocks[i, at, :] = total[i * span : (i + 1) * span]

                @pl.when(lax.rem(me, 2) == 1)
                def _():
                    each = blocks.shape[1]
                    for i in range(rows // each):
                        blocks[shard * (rows // each) + i] = total[i * each : (i + 1) * each]

    for step in range(1, count):
        z_relay(step)
        if step == count - 1:
            outs.open_line()
        if step == 2:
            for keep in keeps:
                keep.wait()
            for hop in range(1, count):
                for turn in range(1, parts):
                    w_across(hop, turn).wait_recv()
        if step >= 2:
            x_relay(step - 2)
            finish(step - 2)
    x_relay(count - 2)
    finish(count - 2)
    x_relay(count - 1)
    finish(count - 1)
    outs.relay(1)
    for hop in range(1, count):
        l_along(hop).wait_recv()
    to_table = pltpu.make_async_copy(lists_all, table, own_sems.at[4])
    to_table.start()
    to_table.wait()
    scale = 1.0 / math.sqrt(own.shape[2])
    attend(count, span, scale, lax.rem(me, 2), table, blocks, own)
    spread(
        count, heads, subs, outs, own, o_all, gate, update, slots, total,
        sz_sems, sx_sems, sc_sems, own_sems.at[5],
    )

    for hop in range(1, count):
        l_along(hop).wait_send()
        w_along(hop, me).wait_send()
        for turn in range(1, parts):
            w_across(hop, turn).wait_send()
    for step in range(count):
        for way in ways(step):
            shard = shard_of(step, way)

            @pl.when(present(step, way))
            def _():
                for chunk in range(chunks):
                    for side in (0, 1) if step == 0 else (way,):
                        @pl.when(onward(side))
                        def _():
                            z_push(shard, chunk, side, False).wait_send()
                    for hop in range(1, heads):
                        x_push(shard, chunk, hop).wait_send()
                    for hop in range(heads):
                        for turn in range(1, subs):
                            c_push(shard, chunk, hop, turn).wait_send()
    for step in range(1, count):
        outs.close_sends(step)
    outs.close_own()


def by_head(hid_own, w_own, o_own, lists, gate, span, block):
    sizes = tuple(lax.axis_size(axis) for axis in ("seq", "groups", "head", "sub"))
    count, parts, heads, subs = sizes
    rows = hid_own.shape[0] * heads * subs
    depth, width = hid_own.shape[1], w_own.shape[1] // count
    chunks = pieces_of(hid_own.shape[0], 4)
    o_chunks = pieces_of(o_own.shape[0] // parts, 2)
    vmem = pl.BlockSpec(memory_space=pltpu.VMEM)
    dma = pltpu.SemaphoreType.DMA
    return pl.pallas_call(
        functools.partial(by_head_kernel, sizes, chunks, o_chunks, span),
        out_shape=jax.ShapeDtypeStruct((rows, o_own.shape[1]), jnp.bfloat16),
        in_specs=[vmem] * 5,
        out_specs=vmem,
        scratch_shapes=[
            pltpu.VMEM((count, rows, depth), jnp.bfloat16),
            pltpu.VMEM((count, w_own.shape[0], width), jnp.bfloat16),
            pltpu.VMEM((count * rows // block, block, width), jnp.bfloat16),
            pltpu.VMEM((count,) + o_own.shape, jnp.bfloat16),
            pltpu.VMEM((count,) + lists.shape, lists.dtype),
            pltpu.SMEM((count,) + lists.shape, lists.dtype),
            pltpu.VMEM((count, rows, width // 3), jnp.bfloat16),
            pltpu.VMEM((heads, subs, rows, count * width // 3), jnp.bfloat16),
            pltpu.VMEM((rows, o_own.shape[1]), jnp.float32),
            dma((parts, 2, count)),
            dma((2, count)),
            dma((2, 2, count, chunks)),
            dma((heads, 2, count, chunks)),
            dma((heads, subs, 2, count, chunks)),
            dma((1 + parts, 2, count, o_chunks)),
            dma((6,)),
            dma((2, count)),
            dma((heads, 2, count)),
            dma((heads, subs, 2, count)),
        ],
        compiler_params=pltpu.CompilerParams(
            collective_id=2, has_side_effects=True, vmem_limit_bytes=56 * 1024 * 1024
        ),
        name="by_head",
    )(hid_own, w_own, o_own, lists, gate)


def attend(count, span, scale, role, table, blocks, out):
    total, block, width = blocks.shape
    size = width // 3
    each = total // count
    slots = each

    def query(b, carry):
        device, row = b // each, lax.rem(b, each)
        used = table[device, each, row]
        q = blocks[b, :, :size]
        numerator = jnp.zeros((block, size), jnp.float32)
        denominator = jnp.zeros((block, 1), jnp.float32)
        for j in range(slots):
            listed = table[device, row, j]
            seen = table[device, row, slots + j]
            at = jnp.where(role == 0, listed, device * each + j)
            alive = jnp.where(role == 0, jnp.where(j < used, 1.0, 0.0), jnp.where(seen > 0, 1.0, 0.0))
            scores = lax.dot_general(
                q, blocks[at, :, size : 2 * size], (((1,), (1,)), ((), ())),
                preferred_element_type=jnp.float32,
            )
            weights = jnp.exp(scores * scale) * alive
            denominator = denominator + jnp.sum(weights, axis=-1, keepdims=True)
            numerator = numerator + jnp.dot(
                weights.astype(jnp.bfloat16), blocks[at, :, 2 * size :],
                preferred_element_type=jnp.float32,
            )
        result = (numerator / denominator).astype(out.dtype)

        @pl.when(role == 0)
        def _():
            at = pl.ds(pl.multiple_of(b * span, span), span)
            for f in range(count):
                out[f, at, :] = result[f * span : (f + 1) * span]

        @pl.when(role == 1)
        def _():
            out[device, pl.ds(pl.multiple_of(row * block, block), block), :] = result

        return carry

    lax.fori_loop(0, total, query, 0, unroll=2)


def spread(
    count, heads, subs, outs, own, w_all, gate, update, slots, total, z_sems, x_sems, c_sems, own_sem
):
    me, head, sub = (lax.axis_index(axis) for axis in ("seq", "head", "sub"))
    size = own.shape[2]

    def columns(step):
        source = lax.rem(me + count - step, count)
        return pl.ds(pl.multiple_of(source * size, size), size)

    def spot(hop, turn, step):
        return slots.at[hop, turn, :, columns(step)]

    def to_seq(step):
        other = lax.rem(me + step, count)
        return push(
            own.at[other], spot(0, 0, 0), z_sems.at[0, step], z_sems.at[1, step], "seq", other
        )

    def to_head(hop, step):
        return push(
            own.at[me] if step == 0 else spot(0, 0, step), spot(hop, 0, step),
            x_sems.at[hop, 0, step], x_sems.at[hop, 1, step],
            "head", lax.rem(head + hop, heads),
        )

    def to_sub(hop, turn, step):
        return push(
            own.at[me] if hop == 0 and step == 0 else spot(hop, 0, step), spot(hop, turn, step),
            c_sems.at[hop, turn, 0, step], c_sems.at[hop, turn, 1, step],
            "sub", lax.rem(sub + turn, subs),
        )

    def hand_over(step):
        for hop in range(1, heads):
            to_head(hop, step).start()
        for turn in range(1, subs):
            to_sub(0, turn, step).start()

    def pass_on(step):
        for hop in range(1, heads):
            to_head(hop, step).wait_recv()
            for turn in range(1, subs):
                to_sub(hop, turn, step).start()

    for step in range(1, count):
        to_seq(step).start()
    hand_over(0)
    keep = pltpu.make_async_copy(own.at[me], spot(0, 0, 0), own_sem)
    keep.start()
    for step in range(1, count):
        if step > 1:
            outs.relay(step)
        to_seq(step).wait_recv()
        hand_over(step)
        pass_on(step - 1)
    keep.wait()

    def add(hop, turn, first):
        owner = lax.rem(head + heads - hop, heads) * subs + lax.rem(sub + subs - turn, subs)
        product = jnp.dot(slots[hop, turn], w_all[owner], preferred_element_type=jnp.float32)
        total[...] = product if first else total[...] + product

    pass_on(count - 1)
    for step in range(1, count):
        for way in (0, 1):
            @pl.when(outs.present(step, way))
            def _():
                outs.complete(outs.shard_of(step, way))
    add(0, 0, True)
    for hop in range(heads):
        if hop:
            add(hop, 0, False)
        for turn in range(1, subs):
            for step in range(count):
                to_sub(hop, turn, step).wait_recv()
            add(hop, turn, False)
    update[...] = (gate[...] * total[...]).astype(update.dtype)
    for step in range(count):
        if step:
            to_seq(step).wait_send()
        for hop in range(1, heads):
            to_head(hop, step).wait_send()
        for hop in range(heads):
            for turn in range(1, subs):
                to_sub(hop, turn, step).wait_send()


def modulate_kernel(tokens, modulation, hidden, held, sem):
    quarter = held.shape[0]
    place = lax.axis_index("head") * lax.axis_size("sub") + lax.axis_index("sub")
    rows = pl.ds(pl.multiple_of(place * quarter, quarter), quarter)
    fetch = pltpu.make_async_copy(tokens.at[rows], held, sem)
    fetch.start()
    fetch.wait()
    gain = 1.0 + modulation[1:2, :]
    shift = modulation[0:1, :]

    def some(i, carry):
        at = pl.ds(pl.multiple_of(i * 16, 16), 16)
        values = held[at, :].astype(jnp.float32)
        centered = values - jnp.mean(values, axis=-1, keepdims=True)
        spread_of = jnp.mean(jnp.square(centered), axis=-1, keepdims=True)
        normed = centered * lax.rsqrt(spread_of + EPSILON)
        hidden[at, :] = (normed * gain + shift).astype(hidden.dtype)
        return carry

    lax.fori_loop(0, quarter // 16, some, 0)


def modulate_part(tokens, modulation, quarter):
    vmem = pl.BlockSpec(memory_space=pltpu.VMEM)
    return pl.pallas_call(
        modulate_kernel,
        out_shape=jax.ShapeDtypeStruct((quarter, tokens.shape[1]), tokens.dtype),
        in_specs=[pl.BlockSpec(memory_space=pl.ANY), vmem],
        out_specs=vmem,
        scratch_shapes=[pltpu.VMEM((quarter, tokens.shape[1]), tokens.dtype), pltpu.SemaphoreType.DMA],
        name="modulate_part",
    )(tokens, modulation)


def shards_by_head(tokens, modulation, w_qkv, w_out, pattern, counts, spatial_mask):
    count = lax.axis_size("seq")
    blocks = lax.axis_size("head") * lax.axis_size("sub")
    row_count = tokens.shape[0]
    depth = w_qkv.shape[0]
    quarter = row_count // blocks
    place = lax.axis_index(("head", "sub"))
    span = BLOCK // count
    hid_own = modulate_part(tokens, modulation, quarter)
    each = counts.shape[0]
    lists = (
        jnp.pad(pattern, ((0, 8 - each), (0, 128 - each)))
        + jnp.pad(counts[None, :], ((each, 7 - each), (0, 128 - each)))
        + jnp.pad(spatial_mask[0], ((0, 8 - each), (each, 128 - 2 * each)))
    )
    out_width = w_out.shape[1]
    gate_slice = lax.dynamic_slice_in_dim(modulation[2], place * out_width, out_width, 0)
    return by_head(
        hid_own, w_qkv.reshape(depth, -1), w_out, lists, gate_slice[None, :], span, BLOCK
    )


def one_head_each(mesh_count, blocks, tokens, w_qkv, pattern, spatial_mask):
    rows, frames = tokens.shape[0], spatial_mask.shape[0]
    return (
        w_qkv.shape[1] * 2 == mesh_count > 2
        and frames == 1
        and mesh_count == blocks
        and pattern.shape[0] == pattern.shape[1] == spatial_mask.shape[1]
        and pattern.shape[0] < 8
        and spatial_mask.shape[2] == pattern.shape[1]
        and rows == BLOCK * spatial_mask.shape[1]
        and BLOCK % (16 * mesh_count) == 0
        and w_qkv.shape[0] % 128 == 0
        and rows % (16 * blocks) == 0
    )


def shards_any(*args):
    tokens, _, w_qkv, _, pattern, _, spatial_mask = args
    blocks = lax.axis_size("head") * lax.axis_size("sub")
    if one_head_each(lax.axis_size("seq"), blocks, tokens, w_qkv, pattern, spatial_mask):
        return shards_by_head(*args)
    return shards(*args)


def solution(mesh):
    return jax.shard_map(
        shards_any,
        mesh=mesh,
        in_specs=(
            P(("groups", "seq"), None),
            P(),
            P("seq", ("head", "sub"), None),
            P("seq", ("head", "sub")),
            P(("groups", "seq"), None),
            P(("groups", "seq")),
            P(("groups", "seq"), None, None),
        ),
        out_specs=P(("groups", "seq"), ("head", "sub")),
        check_vma=False,
    )
```

```python
import functools
import math

import jax
import jax.numpy as jnp
from jax import lax
from jax.experimental import pallas as pl
from jax.experimental.pallas import tpu as pltpu
from jax.sharding import PartitionSpec as P

BLOCK = 128
WIN = 2


EPSILON = 1e-06


def with_halo(cells, sides, width):
    for axis, dim in sides:
        count = lax.axis_size(axis)
        ends = count - 1
        head = lax.slice_in_dim(cells, 0, width, axis=dim)
        tail = lax.slice_in_dim(cells, cells.shape[dim] - width, cells.shape[dim], axis=dim)
        cells = jnp.concatenate(
            [
                lax.ppermute(tail, axis, [(i, (i + 1) % count) for i in range(ends)]),
                cells,
                lax.ppermute(head, axis, [((i + 1) % count, i) for i in range(ends)]),
            ],
            axis=dim,
        )
    return cells


MESH = pl.DeviceIdType.MESH


def pieces_of(rows, most=4):
    for count in range(most, 0, -1):
        if rows % (16 * count) == 0:
            return count
    return 1


class LineGather:
    def __init__(self, own, slots, sems, chunks, count, parts):
        self.own, self.slots, self.chunks = own, slots, chunks
        self.sems, self.count, self.parts = sems, count, parts
        self.me = lax.axis_index("seq")
        self.group = lax.axis_index("groups")
        self.size = own.shape[0] // (parts * chunks)

    def rows(self, group, chunk):
        start = (group * self.chunks + chunk) * self.size
        return pl.ds(pl.multiple_of(start, self.size), self.size)

    def along(self, shard, chunk, way, own):
        rows = self.rows(self.group, chunk)
        source = self.own.at[rows] if own else self.slots.at[shard, rows]
        return pltpu.make_async_remote_copy(
            src_ref=source,
            dst_ref=self.slots.at[shard, rows],
            send_sem=self.sems.at[way, 0, shard, chunk],
            recv_sem=self.sems.at[way, 1, shard, chunk],
            device_id={"seq": self.me + (1 if way == 0 else -1)},
            device_id_type=MESH,
        )

    def across(self, shard, chunk, hop):
        rows = self.rows(self.group, chunk)
        return pltpu.make_async_remote_copy(
            src_ref=self.slots.at[shard, rows],
            dst_ref=self.slots.at[shard, rows],
            send_sem=self.sems.at[1 + hop, 0, shard, chunk],
            recv_sem=self.sems.at[1 + hop, 1, shard, chunk],
            device_id={"groups": lax.rem(self.group + hop, self.parts)},
            device_id_type=MESH,
        )

    def open_line(self):
        for chunk in range(self.chunks):
            for way in (0, 1):
                @pl.when(self.onward(way))
                def _():
                    self.along(self.me, chunk, way, True).start()

    def onward(self, way):
        return self.me < self.count - 1 if way == 0 else self.me > 0

    def shard_of(self, step, way):
        return self.me - step if way == 0 else self.me + step

    def present(self, step, way):
        return self.me >= step if way == 0 else self.me + step < self.count

    def relay(self, step):
        for chunk in range(self.chunks):
            for way in (0, 1):
                shard = self.shard_of(step, way)

                @pl.when(self.present(step, way))
                def _():
                    self.along(shard, chunk, way, False).wait_recv()

                    @pl.when(self.onward(way))
                    def _():
                        self.along(shard, chunk, way, False).start()

                    for hop in range(1, self.parts):
                        self.across(shard, chunk, hop).start()

    def complete(self, shard):
        for chunk in range(self.chunks):
            for hop in range(1, self.parts):
                self.across(shard, chunk, hop).wait_recv()

    def close_sends(self, step):
        for chunk in range(self.chunks):
            for way in (0, 1):
                shard = self.shard_of(step, way)

                @pl.when(self.present(step, way))
                def _():
                    @pl.when(self.onward(way))
                    def _():
                        self.along(shard, chunk, way, False).wait_send()

                    for hop in range(1, self.parts):
                        self.across(shard, chunk, hop).wait_send()

    def close_own(self):
        for chunk in range(self.chunks):
            for way in (0, 1):
                @pl.when(self.onward(way))
                def _():
                    self.along(self.me, chunk, way, True).wait_send()


def project_kernel(count, parts, q_chunks, o_chunks, hidden, w_own, o_own, qkv, o_all, slots, total, q_sems, o_sems, own_sem):
    me = lax.axis_index("seq")
    group = lax.axis_index("groups")
    barrier = pltpu.get_barrier_semaphore()

    @pl.when(me > 0)
    def _():
        pl.semaphore_signal(barrier, inc=1, device_id={"seq": me - 1}, device_id_type=MESH)

    @pl.when(me < count - 1)
    def _():
        pl.semaphore_signal(barrier, inc=1, device_id={"seq": me + 1}, device_id_type=MESH)

    for hop in range(1, parts):
        pl.semaphore_signal(
            barrier, inc=1, device_id={"groups": lax.rem(group + hop, parts)}, device_id_type=MESH
        )
    neighbours = jnp.where(me > 0, 1, 0) + jnp.where(me < count - 1, 1, 0) + (parts - 1)
    pl.semaphore_wait(barrier, neighbours)

    line = LineGather(w_own, slots, q_sems, q_chunks, count, parts)
    outs = LineGather(o_own, o_all, o_sems, o_chunks, count, parts)
    line.open_line()
    keep = pltpu.make_async_copy(o_own, o_all.at[me], own_sem)
    keep.start()
    tile = 256

    def add(shard, block, first):
        def column(j, carry):
            at = pl.ds(pl.multiple_of(j * tile, tile), tile)
            product = jnp.dot(hidden[shard], block[:, at], preferred_element_type=jnp.float32)
            total[:, at] = product if first else total[:, at] + product
            return carry

        lax.fori_loop(0, total.shape[1] // tile, column, 0)

    def finish(step):
        for way in (0, 1):
            shard = line.shard_of(step, way)

            @pl.when(line.present(step, way))
            def _():
                line.complete(shard)
                add(shard, slots.at[shard], False)

    add(me, w_own, True)

    def q_step(step, carry):
        line.relay(step)

        @pl.when(step > 1)
        def _():
            finish(step - 1)

        return carry

    lax.fori_loop(1, count, q_step, 0)
    outs.open_line()
    finish(count - 1)
    qkv[...] = total[...].astype(qkv.dtype)

    def o_step(step, carry):
        outs.relay(step)
        return carry

    lax.fori_loop(1, count, o_step, 0)

    def last(step, carry):
        line.close_sends(step)
        outs.close_sends(step)
        for way in (0, 1):
            shard = outs.shard_of(step, way)

            @pl.when(outs.present(step, way))
            def _():
                outs.complete(shard)

        return carry

    lax.fori_loop(1, count, last, 0)
    line.close_own()
    outs.close_own()
    keep.wait()


def project(hidden, w_own, o_own):
    count, parts = lax.axis_size("seq"), lax.axis_size("groups")
    rows, depth = hidden.shape
    hidden = hidden.reshape(rows, count, depth // count).transpose(1, 0, 2)
    width = w_own.shape[1]
    most = 4 if count <= 8 else 1
    q_chunks = pieces_of(w_own.shape[0] // parts, most)
    o_chunks = pieces_of(o_own.shape[0] // parts, most)
    vmem = pl.BlockSpec(memory_space=pltpu.VMEM)
    return pl.pallas_call(
        functools.partial(project_kernel, count, parts, q_chunks, o_chunks),
        out_shape=[
            jax.ShapeDtypeStruct((rows, width), jnp.bfloat16),
            jax.ShapeDtypeStruct((count,) + o_own.shape, jnp.bfloat16),
        ],
        in_specs=[vmem] * 3,
        out_specs=[vmem, pl.BlockSpec(memory_space=pl.ANY)],
        scratch_shapes=[
            pltpu.VMEM((count,) + w_own.shape, jnp.bfloat16),
            pltpu.VMEM((rows, width), jnp.float32),
            pltpu.SemaphoreType.DMA((1 + parts, 2, count, q_chunks)),
            pltpu.SemaphoreType.DMA((1 + parts, 2, count, o_chunks)),
            pltpu.SemaphoreType.DMA,
        ],
        compiler_params=pltpu.CompilerParams(
            collective_id=0, has_side_effects=True, vmem_limit_bytes=48 * 1024 * 1024
        ),
        name="project",
    )(hidden, w_own, o_own)


def mix_kernel(heads, subs, chunks, attn, w_all, gate, update, slots, total, x_sems, c_sems):
    head, sub = lax.axis_index("head"), lax.axis_index("sub")
    barrier = pltpu.get_barrier_semaphore()
    for hop in range(1, heads):
        pl.semaphore_signal(
            barrier, inc=1, device_id={"head": lax.rem(head + hop, heads)}, device_id_type=MESH
        )
    for hop in range(1, subs):
        pl.semaphore_signal(
            barrier, inc=1, device_id={"sub": lax.rem(sub + hop, subs)}, device_id_type=MESH
        )
    pl.semaphore_wait(barrier, heads + subs - 2)
    size = attn.shape[0] // chunks

    def to_head(hop, chunk):
        rows = pl.ds(chunk * size, size)
        return pltpu.make_async_remote_copy(
            src_ref=attn.at[rows],
            dst_ref=slots.at[hop, 0, rows],
            send_sem=x_sems.at[hop, 0, chunk],
            recv_sem=x_sems.at[hop, 1, chunk],
            device_id={"head": lax.rem(head + hop, heads)},
            device_id_type=MESH,
        )

    def to_sub(hop, turn, chunk):
        rows = pl.ds(chunk * size, size)
        return pltpu.make_async_remote_copy(
            src_ref=attn.at[rows] if hop == 0 else slots.at[hop, 0, rows],
            dst_ref=slots.at[hop, turn, rows],
            send_sem=c_sems.at[hop, turn, 0, chunk],
            recv_sem=c_sems.at[hop, turn, 1, chunk],
            device_id={"sub": lax.rem(sub + turn, subs)},
            device_id_type=MESH,
        )

    for chunk in range(chunks):
        for hop in range(1, heads):
            to_head(hop, chunk).start()
        for turn in range(1, subs):
            to_sub(0, turn, chunk).start()

    def add(chunk, hop, turn, first):
        rows = slice(chunk * size, (chunk + 1) * size)
        owner = lax.rem(head + heads - hop, heads) * subs + lax.rem(sub + subs - turn, subs)
        block = attn[rows, :] if hop == 0 and turn == 0 else slots[hop, turn, rows, :]
        product = jnp.dot(block, w_all[owner], preferred_element_type=jnp.float32)
        total[rows, :] = product if first else total[rows, :] + product

    for chunk in range(chunks):
        add(chunk, 0, 0, True)
    for chunk in range(chunks):
        for turn in range(1, subs):
            to_sub(0, turn, chunk).wait_recv()
            add(chunk, 0, turn, False)
    for chunk in range(chunks):
        for hop in range(1, heads):
            to_head(hop, chunk).wait_recv()
            for turn in range(1, subs):
                to_sub(hop, turn, chunk).start()
            add(chunk, hop, 0, False)
    for chunk in range(chunks):
        for hop in range(1, heads):
            for turn in range(1, subs):
                to_sub(hop, turn, chunk).wait_recv()
                add(chunk, hop, turn, False)
        rows = slice(chunk * size, (chunk + 1) * size)
        update[rows, :] = (gate[...] * total[rows, :]).astype(update.dtype)
    for chunk in range(chunks):
        for hop in range(1, heads):
            to_head(hop, chunk).wait_send()
        for hop in range(heads):
            for turn in range(1, subs):
                to_sub(hop, turn, chunk).wait_send()


def mix(attention, w_all, gate):
    heads, subs = lax.axis_size("head"), lax.axis_size("sub")
    rows, width = attention.shape
    chunks = pieces_of(rows, 2)
    vmem = pl.BlockSpec(memory_space=pltpu.VMEM)
    return pl.pallas_call(
        functools.partial(mix_kernel, heads, subs, chunks),
        out_shape=jax.ShapeDtypeStruct((rows, w_all.shape[-1]), jnp.bfloat16),
        in_specs=[vmem] * 3,
        out_specs=vmem,
        scratch_shapes=[
            pltpu.VMEM((heads, subs, rows, width), jnp.bfloat16),
            pltpu.VMEM((rows, w_all.shape[-1]), jnp.float32),
            pltpu.SemaphoreType.DMA((heads, 2, chunks)),
            pltpu.SemaphoreType.DMA((heads, subs, 2, chunks)),
        ],
        compiler_params=pltpu.CompilerParams(
            collective_id=1, has_side_effects=True, vmem_limit_bytes=40 * 1024 * 1024
        ),
        name="mix",
    )(attention, w_all, gate)


def modulate(tokens, modulation):
    values = tokens.astype(jnp.float32)
    center = jnp.mean(values, axis=-1, keepdims=True)
    spread = jnp.mean(jnp.square(values - center), axis=-1, keepdims=True)
    normed = (values - center) * lax.rsqrt(spread + EPSILON)
    return (normed * (1.0 + modulation[1]) + modulation[0]).astype(jnp.bfloat16)


def shards(tokens, modulation, w_qkv, w_out, pattern, counts, spatial_mask):
    row_count, feature_width = tokens.shape
    pairs_local = w_qkv.shape[1]
    head_size = w_qkv.shape[2] // 6
    frames_local = spatial_mask.shape[0]
    positions = row_count // frames_local
    slot_total = pattern.shape[1]
    scale_factor = 1.0 / math.sqrt(head_size)
    hidden = modulate(tokens, modulation)
    projected, whole_out = project(hidden, w_qkv.reshape(w_qkv.shape[0], -1), w_out)
    packed = projected.reshape(
        frames_local, positions, pairs_local, 6 * head_size
    )
    temporal_in = packed[..., : 3 * head_size].transpose(1, 0, 2, 3)
    received = lax.all_to_all(temporal_in, "seq", split_axis=0, concat_axis=1, tiled=True)
    position_span, frame_total, items, _ = received.shape
    relaid = received.reshape(position_span * frame_total, items, 3 * head_size)
    extended = with_halo(relaid[:, :, head_size:], (("seq", 0),), WIN * BLOCK)
    block_count = position_span * frame_total // BLOCK
    key_table = extended.reshape(block_count + 2 * WIN, BLOCK, items, 2 * head_size)
    queries = relaid[:, :, :head_size].reshape(block_count, BLOCK, items, head_size)
    offsets = pattern - (lax.axis_index("seq") * block_count - WIN)

    def slot_step(slot_index, state_pair):
        numerator, denominator = state_pair
        chosen = lax.dynamic_index_in_dim(offsets, slot_index, 1, keepdims=False)
        picked = jnp.take(key_table, chosen, axis=0)
        scores = (
            jnp.einsum(
                "bqnc,bknc->bnqk",
                queries,
                picked[..., :head_size],
                preferred_element_type=jnp.float32,
            )
            * scale_factor
        )
        alive = (slot_index < counts).astype(jnp.float32)
        weights = jnp.exp(scores) * alive[:, None, None, None]
        numerator = numerator + jnp.einsum(
            "bnqk,bknc->bnqc",
            weights.astype(jnp.bfloat16),
            picked[..., head_size:],
            preferred_element_type=jnp.float32,
        )
        return (numerator, denominator + jnp.sum(weights, axis=-1))

    start_state = (
        jnp.zeros((block_count, items, BLOCK, head_size), jnp.float32),
        jnp.zeros((block_count, items, BLOCK), jnp.float32),
    )
    numerator, denominator = lax.fori_loop(0, slot_total, slot_step, start_state)
    outcome = (numerator / denominator[..., None]).astype(jnp.bfloat16)
    outcome = outcome.transpose(0, 2, 1, 3).reshape(position_span, frame_total, items, head_size)
    temporal_out = lax.all_to_all(outcome, "seq", split_axis=1, concat_axis=0, tiled=True)
    spatial = packed[..., 3 * head_size :]
    blocks_frame = positions // BLOCK
    scores = (
        jnp.einsum(
            "fpnc,fqnc->fnpq",
            spatial[..., :head_size],
            spatial[..., head_size : 2 * head_size],
            preferred_element_type=jnp.float32,
        )
        * scale_factor
    )
    keep = spatial_mask.astype(jnp.float32)[:, None, :, None, :, None]
    weights = (
        jnp.exp(scores).reshape(frames_local, pairs_local, blocks_frame, BLOCK, blocks_frame, BLOCK)
        * keep
    )
    weights = weights.reshape(frames_local, pairs_local, positions, positions)
    denominator = jnp.sum(weights, axis=-1)
    numerator = jnp.einsum(
        "fnpq,fqnc->fpnc",
        weights.astype(jnp.bfloat16),
        spatial[..., 2 * head_size :],
        preferred_element_type=jnp.float32,
    )
    spatial_out = (numerator / denominator.transpose(0, 2, 1)[..., None]).astype(jnp.bfloat16)
    attention = jnp.concatenate([temporal_out.transpose(1, 0, 2, 3), spatial_out], axis=-1)
    attention = attention.reshape(row_count, pairs_local * 2 * head_size)
    out_width = w_out.shape[1]
    blocks = lax.axis_size("head") * lax.axis_size("sub")
    gate_slice = lax.dynamic_slice_in_dim(
        modulation[2], lax.axis_index(("head", "sub")) * out_width, out_width, 0
    )
    return mix(attention, whole_out.reshape(blocks, -1, out_width), gate_slice[None, :])

def meet(axes):
    barrier = pltpu.get_barrier_semaphore()
    others = 0
    for axis in axes:
        size = lax.axis_size(axis)
        for hop in range(1, size):
            other = lax.rem(lax.axis_index(axis) + hop, size)
            pl.semaphore_signal(barrier, inc=1, device_id={axis: other}, device_id_type=MESH)
            others += 1
    pl.semaphore_wait(barrier, others)


def push(source, target, send_sem, recv_sem, axis, place):
    return pltpu.make_async_remote_copy(
        src_ref=source,
        dst_ref=target,
        send_sem=send_sem,
        recv_sem=recv_sem,
        device_id={axis: place},
        device_id_type=MESH,
    )


def by_head_kernel(
    sizes, chunks, o_chunks, span, hid_own, w_own, o_own, lists, gate, update,
    hfull, wfull, blocks, o_all, lists_all, table, own, slots, total,
    w_sems, l_sems, z_sems, x_sems, c_sems, o_sems, own_sems, sz_sems, sx_sems, sc_sems,
):
    count, parts, heads, subs = sizes
    me, group = lax.axis_index("seq"), lax.axis_index("groups")
    head, sub = lax.axis_index("head"), lax.axis_index("sub")
    meet(("seq", "groups", "head", "sub"))
    quarter = hid_own.shape[0]
    size = quarter // chunks
    half = w_own.shape[0] // parts
    width = wfull.shape[2]
    mine = pl.ds(pl.multiple_of(group * half, half), half)

    def place(hop, axis, size_):
        return lax.rem(lax.axis_index(axis) + hop, size_)

    def source_of(hop):
        return lax.rem(me + count - hop, count)

    def w_part(other):
        return pl.ds(pl.multiple_of(other * width, width), width)

    def w_along(hop, shard):
        return push(
            w_own.at[mine, w_part(place(hop, "seq", count))], wfull.at[shard, mine],
            w_sems.at[0, 0, hop], w_sems.at[0, 1, hop], "seq", place(hop, "seq", count),
        )

    def w_across(hop, turn):
        spot = wfull.at[source_of(hop), mine]
        return push(
            spot, spot, w_sems.at[turn, 0, hop], w_sems.at[turn, 1, hop],
            "groups", place(turn, "groups", parts),
        )

    def l_along(hop):
        return push(
            lists, lists_all.at[me], l_sems.at[0, hop], l_sems.at[1, hop],
            "seq", place(hop, "seq", count),
        )

    def rows_of(head_hop, sub_hop, chunk):
        owner = lax.rem(head + heads - head_hop, heads) * subs + lax.rem(sub + subs - sub_hop, subs)
        return pl.ds(pl.multiple_of(owner * quarter + chunk * size, size), size)

    def spot(shard, head_hop, sub_hop, chunk):
        return hfull.at[shard, rows_of(head_hop, sub_hop, chunk)]

    def z_push(shard, chunk, way, own):
        target = spot(shard, 0, 0, chunk)
        return push(
            hid_own.at[pl.ds(chunk * size, size)] if own else target, target,
            z_sems.at[way, 0, shard, chunk], z_sems.at[way, 1, shard, chunk],
            "seq", me + (1 if way == 0 else -1),
        )

    def x_push(shard, chunk, hop, own=False):
        target = spot(shard, 0, 0, chunk)
        return push(
            hid_own.at[pl.ds(chunk * size, size)] if own else target, target,
            x_sems.at[hop, 0, shard, chunk], x_sems.at[hop, 1, shard, chunk],
            "head", place(hop, "head", heads),
        )

    def c_push(shard, chunk, hop, turn, own=False):
        target = spot(shard, hop, 0, chunk)
        return push(
            hid_own.at[pl.ds(chunk * size, size)] if own else target, target,
            c_sems.at[hop, turn, 0, shard, chunk], c_sems.at[hop, turn, 1, shard, chunk],
            "sub", place(turn, "sub", subs),
        )

    outs = LineGather(o_own, o_all, o_sems, o_chunks, count, parts)
    onward, shard_of, present = outs.onward, outs.shard_of, outs.present
    ways = lambda step: (0, 1) if step else (0,)

    for hop in range(1, count):
        l_along(hop).start()
    for hop in range(1, count):
        w_along(hop, me).start()
    for chunk in range(chunks):
        for way in (0, 1):
            @pl.when(onward(way))
            def _():
                z_push(me, chunk, way, True).start()
        for hop in range(1, heads):
            x_push(me, chunk, hop, True).start()
        for turn in range(1, subs):
            c_push(me, chunk, 0, turn, True).start()
    keeps = [
        pltpu.make_async_copy(o_own, o_all.at[me], own_sems.at[0]),
        pltpu.make_async_copy(w_own.at[:, w_part(me)], wfull.at[me], own_sems.at[1]),
        pltpu.make_async_copy(
            hid_own,
            hfull.at[me, pl.ds(pl.multiple_of((head * subs + sub) * quarter, quarter), quarter)],
            own_sems.at[2],
        ),
        pltpu.make_async_copy(lists, lists_all.at[me], own_sems.at[3]),
    ]
    for keep in keeps:
        keep.start()

    for hop in range(1, count):
        w_along(hop, source_of(hop)).wait_recv()
        for turn in range(1, parts):
            w_across(hop, turn).start()

    def z_relay(step):
        for chunk in range(chunks):
            for way in ways(step):
                shard = shard_of(step, way)

                @pl.when(present(step, way))
                def _():
                    z_push(shard, chunk, way, False).wait_recv()

                    @pl.when(onward(way))
                    def _():
                        z_push(shard, chunk, way, False).start()

                    for hop in range(1, heads):
                        x_push(shard, chunk, hop).start()
                    for turn in range(1, subs):
                        c_push(shard, chunk, 0, turn).start()

    def x_relay(step):
        for chunk in range(chunks):
            for way in ways(step):
                shard = shard_of(step, way)

                @pl.when(present(step, way))
                def _():
                    for hop in range(1, heads):
                        x_push(shard, chunk, hop).wait_recv()
                        for turn in range(1, subs):
                            c_push(shard, chunk, hop, turn).start()

    def finish(step):
        for way in ways(step):
            shard = shard_of(step, way)

            @pl.when(present(step, way))
            def _():
                for chunk in range(chunks):
                    for hop in range(heads):
                        for turn in range(1, subs):
                            c_push(shard, chunk, hop, turn).wait_recv()
                weight = wfull[...].reshape(-1, wfull.shape[-1])
                total = jnp.dot(hfull[shard], weight, preferred_element_type=jnp.float32)
                total = total.astype(blocks.dtype)
                rows = total.shape[0]

                @pl.when(lax.rem(me, 2) == 0)
                def _():
                    at = pl.ds(pl.multiple_of(shard * span, span), span)
                    for i in range(rows // span):
                        blocks[i, at, :] = total[i * span : (i + 1) * span]

                @pl.when(lax.rem(me, 2) == 1)
                def _():
                    each = blocks.shape[1]
                    for i in range(rows // each):
                        blocks[shard * (rows // each) + i] = total[i * each : (i + 1) * each]

    for step in range(1, count):
        z_relay(step)
        if step == count - 1:
            outs.open_line()
        if step == 2:
            for keep in keeps:
                keep.wait()
            for hop in range(1, count):
                for turn in range(1, parts):
                    w_across(hop, turn).wait_recv()
        if step >= 2:
            x_relay(step - 2)
            finish(step - 2)
    x_relay(count - 2)
    finish(count - 2)
    x_relay(count - 1)
    finish(count - 1)
    outs.relay(1)
    for hop in range(1, count):
        l_along(hop).wait_recv()
    to_table = pltpu.make_async_copy(lists_all, table, own_sems.at[4])
    to_table.start()
    to_table.wait()
    scale = 1.0 / math.sqrt(own.shape[2])
    attend(count, span, scale, lax.rem(me, 2), table, blocks, own)
    spread(
        count, heads, subs, outs, own, o_all, gate, update, slots, total,
        sz_sems, sx_sems, sc_sems, own_sems.at[5],
    )

    for hop in range(1, count):
        l_along(hop).wait_send()
        w_along(hop, me).wait_send()
        for turn in range(1, parts):
            w_across(hop, turn).wait_send()
    for step in range(count):
        for way in ways(step):
            shard = shard_of(step, way)

            @pl.when(present(step, way))
            def _():
                for chunk in range(chunks):
                    for side in (0, 1) if step == 0 else (way,):
                        @pl.when(onward(side))
                        def _():
                            z_push(shard, chunk, side, False).wait_send()
                    for hop in range(1, heads):
                        x_push(shard, chunk, hop).wait_send()
                    for hop in range(heads):
                        for turn in range(1, subs):
                            c_push(shard, chunk, hop, turn).wait_send()
    for step in range(1, count):
        outs.close_sends(step)
    outs.close_own()


def by_head(hid_own, w_own, o_own, lists, gate, span, block):
    sizes = tuple(lax.axis_size(axis) for axis in ("seq", "groups", "head", "sub"))
    count, parts, heads, subs = sizes
    rows = hid_own.shape[0] * heads * subs
    depth, width = hid_own.shape[1], w_own.shape[1] // count
    chunks = pieces_of(hid_own.shape[0], 4)
    o_chunks = pieces_of(o_own.shape[0] // parts, 2)
    vmem = pl.BlockSpec(memory_space=pltpu.VMEM)
    dma = pltpu.SemaphoreType.DMA
    return pl.pallas_call(
        functools.partial(by_head_kernel, sizes, chunks, o_chunks, span),
        out_shape=jax.ShapeDtypeStruct((rows, o_own.shape[1]), jnp.bfloat16),
        in_specs=[vmem] * 5,
        out_specs=vmem,
        scratch_shapes=[
            pltpu.VMEM((count, rows, depth), jnp.bfloat16),
            pltpu.VMEM((count, w_own.shape[0], width), jnp.bfloat16),
            pltpu.VMEM((count * rows // block, block, width), jnp.bfloat16),
            pltpu.VMEM((count,) + o_own.shape, jnp.bfloat16),
            pltpu.VMEM((count,) + lists.shape, lists.dtype),
            pltpu.SMEM((count,) + lists.shape, lists.dtype),
            pltpu.VMEM((count, rows, width // 3), jnp.bfloat16),
            pltpu.VMEM((heads, subs, rows, count * width // 3), jnp.bfloat16),
            pltpu.VMEM((rows, o_own.shape[1]), jnp.float32),
            dma((parts, 2, count)),
            dma((2, count)),
            dma((2, 2, count, chunks)),
            dma((heads, 2, count, chunks)),
            dma((heads, subs, 2, count, chunks)),
            dma((1 + parts, 2, count, o_chunks)),
            dma((6,)),
            dma((2, count)),
            dma((heads, 2, count)),
            dma((heads, subs, 2, count)),
        ],
        compiler_params=pltpu.CompilerParams(
            collective_id=2, has_side_effects=True, vmem_limit_bytes=56 * 1024 * 1024
        ),
        name="by_head",
    )(hid_own, w_own, o_own, lists, gate)


def attend(count, span, scale, role, table, blocks, out):
    total, block, width = blocks.shape
    size = width // 3
    each = total // count
    slots = each

    def query(b, carry):
        device, row = b // each, lax.rem(b, each)
        used = table[device, each, row]
        q = blocks[b, :, :size]
        numerator = jnp.zeros((block, size), jnp.float32)
        denominator = jnp.zeros((block, 1), jnp.float32)
        for j in range(slots):
            listed = table[device, row, j]
            seen = table[device, row, slots + j]
            at = jnp.where(role == 0, listed, device * each + j)
            alive = jnp.where(role == 0, jnp.where(j < used, 1.0, 0.0), jnp.where(seen > 0, 1.0, 0.0))
            scores = lax.dot_general(
                q, blocks[at, :, size : 2 * size], (((1,), (1,)), ((), ())),
                preferred_element_type=jnp.float32,
            )
            weights = jnp.exp(scores * scale) * alive
            denominator = denominator + jnp.sum(weights, axis=-1, keepdims=True)
            numerator = numerator + jnp.dot(
                weights.astype(jnp.bfloat16), blocks[at, :, 2 * size :],
                preferred_element_type=jnp.float32,
            )
        result = (numerator / denominator).astype(out.dtype)

        @pl.when(role == 0)
        def _():
            at = pl.ds(pl.multiple_of(b * span, span), span)
            for f in range(count):
                out[f, at, :] = result[f * span : (f + 1) * span]

        @pl.when(role == 1)
        def _():
            out[device, pl.ds(pl.multiple_of(row * block, block), block), :] = result

        return carry

    lax.fori_loop(0, total, query, 0, unroll=2)


def spread(
    count, heads, subs, outs, own, w_all, gate, update, slots, total, z_sems, x_sems, c_sems, own_sem
):
    me, head, sub = (lax.axis_index(axis) for axis in ("seq", "head", "sub"))
    size = own.shape[2]

    def columns(step):
        source = lax.rem(me + count - step, count)
        return pl.ds(pl.multiple_of(source * size, size), size)

    def spot(hop, turn, step):
        return slots.at[hop, turn, :, columns(step)]

    def to_seq(step):
        other = lax.rem(me + step, count)
        return push(
            own.at[other], spot(0, 0, 0), z_sems.at[0, step], z_sems.at[1, step], "seq", other
        )

    def to_head(hop, step):
        return push(
            own.at[me] if step == 0 else spot(0, 0, step), spot(hop, 0, step),
            x_sems.at[hop, 0, step], x_sems.at[hop, 1, step],
            "head", lax.rem(head + hop, heads),
        )

    def to_sub(hop, turn, step):
        return push(
            own.at[me] if hop == 0 and step == 0 else spot(hop, 0, step), spot(hop, turn, step),
            c_sems.at[hop, turn, 0, step], c_sems.at[hop, turn, 1, step],
            "sub", lax.rem(sub + turn, subs),
        )

    def hand_over(step):
        for hop in range(1, heads):
            to_head(hop, step).start()
        for turn in range(1, subs):
            to_sub(0, turn, step).start()

    def pass_on(step):
        for hop in range(1, heads):
            to_head(hop, step).wait_recv()
            for turn in range(1, subs):
                to_sub(hop, turn, step).start()

    for step in range(1, count):
        to_seq(step).start()
    hand_over(0)
    keep = pltpu.make_async_copy(own.at[me], spot(0, 0, 0), own_sem)
    keep.start()
    for step in range(1, count):
        if step > 1:
            outs.relay(step)
        to_seq(step).wait_recv()
        hand_over(step)
        pass_on(step - 1)
    keep.wait()

    def add(hop, turn, first):
        owner = lax.rem(head + heads - hop, heads) * subs + lax.rem(sub + subs - turn, subs)
        product = jnp.dot(slots[hop, turn], w_all[owner], preferred_element_type=jnp.float32)
        total[...] = product if first else total[...] + product

    pass_on(count - 1)
    for step in range(1, count):
        for way in (0, 1):
            @pl.when(outs.present(step, way))
            def _():
                outs.complete(outs.shard_of(step, way))
    add(0, 0, True)
    for hop in range(heads):
        if hop:
            add(hop, 0, False)
        for turn in range(1, subs):
            for step in range(count):
                to_sub(hop, turn, step).wait_recv()
            add(hop, turn, False)
    update[...] = (gate[...] * total[...]).astype(update.dtype)
    for step in range(count):
        if step:
            to_seq(step).wait_send()
        for hop in range(1, heads):
            to_head(hop, step).wait_send()
        for hop in range(heads):
            for turn in range(1, subs):
                to_sub(hop, turn, step).wait_send()


def modulate_kernel(tokens, modulation, hidden, held, sem):
    quarter = held.shape[0]
    place = lax.axis_index("head") * lax.axis_size("sub") + lax.axis_index("sub")
    rows = pl.ds(pl.multiple_of(place * quarter, quarter), quarter)
    fetch = pltpu.make_async_copy(tokens.at[rows], held, sem)
    fetch.start()
    fetch.wait()
    gain = 1.0 + modulation[1:2, :]
    shift = modulation[0:1, :]

    def some(i, carry):
        at = pl.ds(pl.multiple_of(i * 16, 16), 16)
        values = held[at, :].astype(jnp.float32)
        centered = values - jnp.mean(values, axis=-1, keepdims=True)
        spread_of = jnp.mean(jnp.square(centered), axis=-1, keepdims=True)
        normed = centered * lax.rsqrt(spread_of + EPSILON)
        hidden[at, :] = (normed * gain + shift).astype(hidden.dtype)
        return carry

    lax.fori_loop(0, quarter // 16, some, 0, unroll=4)


def modulate_part(tokens, modulation, quarter):
    vmem = pl.BlockSpec(memory_space=pltpu.VMEM)
    return pl.pallas_call(
        modulate_kernel,
        out_shape=jax.ShapeDtypeStruct((quarter, tokens.shape[1]), tokens.dtype),
        in_specs=[pl.BlockSpec(memory_space=pl.ANY), vmem],
        out_specs=vmem,
        scratch_shapes=[pltpu.VMEM((quarter, tokens.shape[1]), tokens.dtype), pltpu.SemaphoreType.DMA],
        name="modulate_part",
    )(tokens, modulation)


def shards_by_head(tokens, modulation, w_qkv, w_out, pattern, counts, spatial_mask):
    count = lax.axis_size("seq")
    blocks = lax.axis_size("head") * lax.axis_size("sub")
    row_count = tokens.shape[0]
    depth = w_qkv.shape[0]
    quarter = row_count // blocks
    place = lax.axis_index(("head", "sub"))
    span = BLOCK // count
    hid_own = modulate_part(tokens, modulation, quarter)
    each = counts.shape[0]
    lists = (
        jnp.pad(pattern, ((0, 8 - each), (0, 128 - each)))
        + jnp.pad(counts[None, :], ((each, 7 - each), (0, 128 - each)))
        + jnp.pad(spatial_mask[0], ((0, 8 - each), (each, 128 - 2 * each)))
    )
    out_width = w_out.shape[1]
    gate_slice = lax.dynamic_slice_in_dim(modulation[2], place * out_width, out_width, 0)
    return by_head(
        hid_own, w_qkv.reshape(depth, -1), w_out, lists, gate_slice[None, :], span, BLOCK
    )


def one_head_each(mesh_count, blocks, tokens, w_qkv, pattern, spatial_mask):
    rows, frames = tokens.shape[0], spatial_mask.shape[0]
    return (
        w_qkv.shape[1] * 2 == mesh_count > 2
        and frames == 1
        and mesh_count == blocks
        and pattern.shape[0] == pattern.shape[1] == spatial_mask.shape[1]
        and pattern.shape[0] < 8
        and spatial_mask.shape[2] == pattern.shape[1]
        and rows == BLOCK * spatial_mask.shape[1]
        and BLOCK % (16 * mesh_count) == 0
        and w_qkv.shape[0] % 128 == 0
        and rows % (16 * blocks) == 0
    )


def shards_any(*args):
    tokens, _, w_qkv, _, pattern, _, spatial_mask = args
    blocks = lax.axis_size("head") * lax.axis_size("sub")
    if one_head_each(lax.axis_size("seq"), blocks, tokens, w_qkv, pattern, spatial_mask):
        return shards_by_head(*args)
    return shards(*args)


def solution(mesh):
    return jax.shard_map(
        shards_any,
        mesh=mesh,
        in_specs=(
            P(("groups", "seq"), None),
            P(),
            P("seq", ("head", "sub"), None),
            P("seq", ("head", "sub")),
            P(("groups", "seq"), None),
            P(("groups", "seq")),
            P(("groups", "seq"), None, None),
        ),
        out_specs=P(("groups", "seq"), ("head", "sub")),
        check_vma=False,
    )
```
